32 devices in a mesh: expert: 4 (over y, core), dp: 8 (over z, x).
Axes of the slice: x: 2, y: 2, z: 4, core: 2. Of those that a mesh axis runs over, the one named last changes fastest.
Arguments:
- tokens: bfloat16 [4096, 4096], P(('expert', 'dp')), may hold values from -6 to 6
- gates: float32 [4096, 8], P(('expert', 'dp')), may hold values from 0.05 to 1
- routes: int32 [4096, 8], P(('expert', 'dp')), may hold values from 0 to 63, all different within a row; in each aligned block of 128 rows (0 to 127, 128 to 255, ...) at most 32 rows name the same one
- doc_ids: int32 [4096], P(('expert', 'dp')), may hold values from 0 to 1
- hidden_grad: bfloat16 [64, 1024, 1536], P('expert', 'dp'), may hold values from -6 to 6
- proj_in: bfloat16 [4096, 64], replicated, may hold values from -0.09375 to 0.09375
- proj_out: bfloat16 [64, 1536, 64], P('expert'), may hold values from -0.15625 to 0.15625
- val_features: bfloat16 [32, 64, 4096], P('dp', 'expert'), may hold values from -6 to 6
Outputs:
- scores: float32 [16, 32], P('dp')
The draws below stay inside these ranges and needn't reach their ends.
Inputs may be any that keep to these rules, and one draw needn't show every extreme that they name: Each row names 8 different experts; among the rows of one device no expert is named by more than 32 routes, and in every draw some expert by exactly 32.
All inputs are finite; a program needn't handle non-finite values.
Results may differ from the reference program's by a relative error of at most 0.0049.
Values may be sent and summed in bfloat16 or wider, within the bound.
No kernel may reach another device: no remote copies, remote signals or barrier semaphores. Data moves between devices by JAX's collectives and lax.ppermute only.
A program may use at most 64 MiB of HBM per device.

```python
import math
import jax
import jax.numpy as jnp
import numpy as np
from jax import lax

D = 4096
FF = 1536
EXPERTS = 64
TOPK = 8
RANK = 64
TOK_DEV = 128
CAP = 32
DOC_GRP = 2
VAL = 32
N_EXPERT = 4
N_DP = 8


def set_ends(entries, own_key, low, largest):
    longest = entries.shape.index(max(entries.shape))
    spots = []
    for shift in (0, 1):
        where = [jax.random.randint(jax.random.fold_in(own_key, axis), (), 0, length) for axis, length in enumerate(entries.shape)]
        where[longest] = (where[longest] + shift) % entries.shape[longest]
        spots.append(tuple(where))
    return entries.at[spots[0]].set(low).at[spots[1]].set(largest)


def level_of(rng, extent, split, smallest, top_value):
    def one(dim, blocks):
        draws = jax.random.uniform(jax.random.fold_in(jax.random.fold_in(rng, 6), dim), (blocks,), jnp.float32, smallest / len(split), top_value / len(split))
        return jnp.repeat(jnp.exp(draws), extent[dim] // blocks).reshape((-1,) + (1,) * (len(extent) - dim - 1))

    level = one(*split[0])
    for cut in split[1:]:
        level = level * one(*cut)
    return level


def shared_out(stream_key, own, number, rows, number_of, top, reach, slope):
    sequence = jax.random.permutation(stream_key, number_of)
    crowded, usual = load_shares(number_of, rows * top, reach, slope, True), load_shares(number_of, rows * top, reach, slope, False)
    places = jnp.arange(number_of)

    def named(tallies, rotation):
        used = int((tallies > 0).sum())
        fixed = max(1, used // 4)
        passed = fixed + (places - fixed + rotation * (used - fixed)) % max(1, number_of - fixed)
        return jnp.zeros((number_of,), jnp.int32).at[sequence[jnp.where(places < fixed, places, passed)]].set(jnp.asarray(tallies, jnp.int32))

    tallies = jnp.where(number % 4 == 0, named(crowded, number // 4), named(usual, number - number // 4 - 1))
    mixed = jax.random.permutation(jax.random.fold_in(own, 3), number_of)
    giver, taker = mixed[0:number_of // 2 * 2:2], mixed[1:number_of // 2 * 2:2]
    slack = jnp.minimum(tallies[giver] - 1, reach - tallies[taker]) // 2
    slack = jnp.where((giver == sequence[0]) | (taker == sequence[0]) | (tallies[taker] == 0), 0, jnp.maximum(slack, 0))
    passed = jax.random.randint(jax.random.fold_in(own, 4), (number_of // 2,), 0, 1 << 20) % (slack + 1)
    tallies = tallies.at[giver].add(-passed).at[taker].add(passed)
    labels = jnp.searchsorted(jnp.cumsum(tallies), jnp.arange(rows * top), side="right").astype(jnp.int32)
    table = labels.reshape(top, rows).T
    table = table[jax.random.permutation(jax.random.fold_in(own, 1), rows)]
    rotation = jax.random.randint(jax.random.fold_in(own, 2), (rows, 1), 0, top)
    return jnp.take_along_axis(table, (jnp.arange(top)[None, :] + rotation) % top, axis=1)


def load_shares(amount, total, bound, lean, full):
    portions = [(1 << 20) // math.isqrt(grade ** lean) + 1 for grade in range(1, amount + 1)]
    largest = bound if full else min(bound, max(-(-total // amount), total * portions[0] // sum(portions)))
    least = 1 if total - largest >= amount - 1 else 0
    holding, rest = [largest] + [least] * (amount - 1), total - largest - least * (amount - 1)
    while rest > 0:
        movable = [i for i in range(1, amount) if holding[i] < largest] or [i for i in range(1, amount) if holding[i] < bound]
        mass, budget = sum([portions[i] for i in movable]), rest
        for i in movable:
            extra = min(bound - holding[i], max(1, budget * portions[i] // mass), rest)
            holding[i] = holding[i] + extra
            rest = rest - extra
    return np.array(holding)


def gaussian(key, extent, scale, bound, cuts=(), kind=jnp.bfloat16):
    values = scale * jax.random.normal(key, extent, jnp.float32)
    if cuts:
        values = values * level_of(key, extent, cuts, -0.22, 0.18)
    return jnp.clip(values, -bound, bound).astype(kind)


def setup_inputs(seed: int = 0) -> dict:
    keys = jax.random.split(jax.random.key(seed), 9)
    tokens = gaussian(keys[0], (N_EXPERT * N_DP * TOK_DEV, D), 1.0, 6.0, ((0, 32),))
    gates = jnp.clip(jnp.exp(math.log(1.0) - 2.9957323 * jax.random.uniform(keys[1], (N_EXPERT * N_DP * TOK_DEV, TOPK), jnp.float32) ** level_of(keys[1], (N_EXPERT * N_DP * TOK_DEV, TOPK), ((0, 32),), -0.2, 0.2)), 0.05, 1.0)
    routes_keys = jax.random.split(jax.random.fold_in(keys[2], 1), (N_EXPERT * N_DP * TOK_DEV) // TOK_DEV)
    routes_turns = jax.random.permutation(jax.random.fold_in(keys[2], 3), (N_EXPERT * N_DP * TOK_DEV) // TOK_DEV)
    routes = jax.vmap(lambda own, number: shared_out(jax.random.fold_in(keys[2], 2), own, number, TOK_DEV, EXPERTS, TOPK, CAP, 2))(routes_keys, routes_turns).reshape((N_EXPERT * N_DP * TOK_DEV, TOPK))
    doc_ids = set_ends(jax.random.randint(keys[3], (N_EXPERT * N_DP * TOK_DEV,), 0, DOC_GRP), jax.random.fold_in(keys[3], 1), 0, DOC_GRP - 1).astype(jnp.int32)
    hidden_grad = gaussian(keys[4], (EXPERTS, N_DP * N_EXPERT * CAP, FF), 1.0, 6.0, ((0, 4), (1, 8)))
    proj_in = gaussian(keys[5], (D, RANK), D ** -0.5, 0.09375)
    proj_out = gaussian(keys[6], (EXPERTS, FF, RANK), FF ** -0.5, 0.15625, ((0, 4),))
    val_features = gaussian(keys[7], (VAL, EXPERTS, RANK * RANK), 1.0, 6.0, ((0, 8), (1, 4)))
    return dict(tokens=tokens, gates=gates, routes=routes, doc_ids=doc_ids, hidden_grad=hidden_grad, proj_in=proj_in, proj_out=proj_out, val_features=val_features)


def slot_of(block):
    onehot = (block[:, None] == jnp.arange(EXPERTS, dtype=jnp.int32)[None, :]).astype(jnp.int32)
    prior = jnp.cumsum(onehot, axis=0) - onehot
    return lax.optimization_barrier(jnp.sum(prior * onehot, axis=1)).astype(jnp.int32)

def expert_features(items):
    grad_rows, proj_rows, acts, owners = items
    lowered = jnp.dot(grad_rows, proj_rows, preferred_element_type=jnp.float32).astype(jnp.bfloat16)
    member = (owners[:, None] == jnp.arange(DOC_GRP, dtype=jnp.int32)[None, :]).astype(jnp.float32)
    member = member.reshape(N_DP, N_EXPERT * CAP, DOC_GRP)
    left = acts.astype(jnp.float32).reshape(N_DP, N_EXPERT * CAP, RANK)
    right = lowered.astype(jnp.float32).reshape(N_DP, N_EXPERT * CAP, RANK)
    spread = (member[:, :, :, None] * left[:, :, None, :]).reshape(N_DP, N_EXPERT * CAP, DOC_GRP * RANK)
    feats = jnp.einsum('grm,grb->gmb', spread, right)
    return feats.reshape(N_DP, DOC_GRP, RANK * RANK).astype(jnp.bfloat16)

def reference(tokens, gates, routes, doc_ids, hidden_grad, proj_in, proj_out, val_features):
    total = tokens.shape[0]
    rows = N_DP * N_EXPERT * CAP
    act = jnp.dot(tokens, proj_in, preferred_element_type=jnp.float32)
    sent = (gates[:, :, None] * act[:, None, :]).astype(jnp.bfloat16)
    slots = lax.map(slot_of, routes.reshape(N_EXPERT * N_DP, TOK_DEV * TOPK)).reshape(total, TOPK)
    device = jnp.arange(total, dtype=jnp.int32) // TOK_DEV
    source = device // N_DP
    group = device % N_DP
    row = group[:, None] * (N_EXPERT * CAP) + source[:, None] * CAP + slots
    index = (routes * rows + row).reshape(-1).astype(jnp.int32)
    filled = jnp.zeros((EXPERTS * rows, RANK), jnp.bfloat16).at[index].set(sent.reshape(-1, RANK))
    owner_ids = jnp.full((EXPERTS * rows,), DOC_GRP, jnp.int32).at[index].set(jnp.repeat(doc_ids, TOPK).astype(jnp.int32))
    feats = lax.map(expert_features, (hidden_grad, proj_out, filled.reshape(EXPERTS, rows, RANK), owner_ids.reshape(EXPERTS, rows)))
    flat = jnp.transpose(feats, (1, 2, 0, 3)).reshape(N_DP * DOC_GRP, EXPERTS * RANK * RANK)
    vals = val_features.reshape(val_features.shape[0], EXPERTS * RANK * RANK)
    total_scores = lax.dot_general(flat, vals, (((1,), (1,)), ((), ())), preferred_element_type=jnp.float32)
    return total_scores / jnp.sqrt(jnp.float32(EXPERTS * RANK * RANK))
```

```python
import functools

import jax
import jax.numpy as jnp
from jax import lax
from jax.experimental import pallas as pl
from jax.experimental.pallas import tpu as pltpu
from jax.sharding import PartitionSpec as P

DOC_GRP = 2
LANES = 128
F32 = jnp.float32
BF16 = jnp.bfloat16
NT = (((1,), (1,)), ((), ()))
TN = (((0,), (0,)), ((), ()))


def act_kernel(tok_ref, proj_ref, routes_ref, gates_ref, docs_ref, out_ref, acc_ref):
    rank = proj_ref.shape[0]
    top = routes_ref.shape[0]
    half = rank // 2
    step = pl.program_id(0)

    @pl.when(step == 0)
    def _():
        acc_ref[...] = jnp.zeros_like(acc_ref)

    acc_ref[...] += lax.dot_general(proj_ref[...], tok_ref[...], NT, preferred_element_type=F32)

    @pl.when(step == pl.num_programs(0) - 1)
    def _():
        out_ref[0:half, :] = acc_ref[pl.ds(0, half, stride=2), :]
        out_ref[half:rank, :] = acc_ref[pl.ds(1, half, stride=2), :]
        out_ref[rank : rank + top, :] = routes_ref[...].astype(F32)
        out_ref[rank + top : rank + 2 * top, :] = gates_ref[...]
        out_ref[rank + 2 * top :, :] = jnp.broadcast_to(
            docs_ref[...].astype(F32), (out_ref.shape[0] - rank - 2 * top, out_ref.shape[1])
        )


def lowered_kernel(grad_ref, proj_ref, out_ref):
    for e in range(grad_ref.shape[0]):
        low = lax.dot_general(grad_ref[e], proj_ref[e], NT, preferred_element_type=F32)
        out_ref[e] = jnp.concatenate([low, low], axis=1).astype(BF16)


def feature_kernel(groups, rank, top, me_ref, *refs):
    pays, low_ref, out_ref, a_ref, f_ref = refs[:groups], *refs[groups:]
    exp_local, rows, _ = low_ref.shape
    cap = rows // groups
    tok = pays[0].shape[1]
    half = rank // 2
    me = me_ref[0]
    base = (me * exp_local).astype(F32)
    experts = lax.broadcasted_iota(jnp.int32, (exp_local, tok), 0).astype(F32) + base
    before = (
        lax.broadcasted_iota(jnp.int32, (tok, tok), 0)
        < lax.broadcasted_iota(jnp.int32, (tok, tok), 1)
    ).astype(BF16)
    slots = lax.broadcasted_iota(jnp.int32, (cap, tok), 0).astype(F32)
    for k in range(groups):
        pay = pays[k]
        hit = jnp.zeros((exp_local, tok), F32)
        gate = jnp.zeros((exp_local, tok), F32)
        for t in range(top):
            same = pay[rank + t : rank + t + 1, :] == experts
            hit = jnp.where(same, 1.0, hit)
            gate = jnp.where(same, pay[rank + top + t : rank + top + t + 1, :], gate)
        slot = jnp.dot(hit.astype(BF16), before, preferred_element_type=F32)
        slot = jnp.where(hit > 0.0, slot, -1.0)
        doc = pay[rank + 2 * top : rank + 2 * top + 1, :]
        parts = []
        for par in range(2):
            act = pay[par * half : (par + 1) * half, :]
            for d in range(DOC_GRP):
                parts.append(jnp.where(doc == float(d), act, 0.0))
        act = jnp.concatenate(parts, axis=0)
        high = act.astype(BF16)
        low = (act - high.astype(F32)).astype(BF16)
        right = jnp.concatenate([high, low], axis=1)
        picks, scales = [], []
        for e in range(exp_local):
            pick = slot[e : e + 1, :] == slots
            picks.append(jnp.where(pick, 1.0, 0.0).astype(BF16))
            scales.append(
                jnp.sum(jnp.where(pick, gate[e : e + 1, :], 0.0), axis=1, keepdims=True)
            )
        left = jnp.concatenate(picks, axis=0)
        scale = jnp.concatenate(scales, axis=0)
        left = jnp.concatenate([left, left], axis=1)
        sent = lax.dot_general(left, right, NT, preferred_element_type=F32) * scale
        sent = sent.astype(BF16)
        source = pl.multiple_of(lax.bitwise_xor(me, k) * cap, cap)
        for e in range(exp_local):
            a_ref[e, pl.ds(source, cap), :] = sent[e * cap : (e + 1) * cap, :]
    wide = DOC_GRP * half
    lane = lax.broadcasted_iota(jnp.int32, (wide, 2 * rank), 1)
    for e in range(exp_local):
        feat = lax.dot_general(a_ref[e], low_ref[e], TN, preferred_element_type=F32)
        f_ref[pl.ds(e, wide, stride=exp_local), :] = jnp.where(
            lane < rank, feat[:wide], feat[wide:]
        )
    parts, _, chunks, _, _ = out_ref.shape
    size = chunks * exp_local
    for d in range(DOC_GRP):
        for p in range(parts):
            start = (d * half + p * chunks) * exp_local
            out_ref[p, d] = (
                f_ref[start : start + size, :].astype(BF16).reshape(chunks, exp_local, 2 * rank)
            )


def score_kernel(scale, feat_ref, val_ref, out_ref):
    dp, docs, chunks, exp_local, lanes = feat_ref.shape
    vals = val_ref.shape[1]
    left_rows, right_rows = dp * docs * exp_local, dp * vals * exp_local
    total = jnp.zeros((left_rows, right_rows), F32)
    for c in range(chunks):
        left = feat_ref[:, :, c].reshape(left_rows, lanes)
        right = val_ref[:, :, :, c * lanes : (c + 1) * lanes].reshape(right_rows, lanes)
        total += lax.dot_general(left, right, NT, preferred_element_type=F32)
    row = lax.broadcasted_iota(jnp.int32, total.shape, 0) % exp_local
    col = lax.broadcasted_iota(jnp.int32, total.shape, 1) % exp_local
    total = jnp.where(row == col, total, 0.0)
    total = jnp.sum(total.reshape(dp * docs, exp_local, right_rows), axis=1)
    pick = (
        lax.broadcasted_iota(jnp.int32, (right_rows, dp * vals), 0) // exp_local
        == lax.broadcasted_iota(jnp.int32, (right_rows, dp * vals), 1)
    ).astype(F32)
    scores = jnp.dot(
        total, pick, preferred_element_type=F32, precision=lax.Precision.HIGHEST
    ) * scale
    for i in range(out_ref.shape[0] // dp):
        for j in range(dp):
            out_ref[i * dp + j] = scores[j * docs : (j + 1) * docs, :]


def body(tokens, gates, routes, doc_ids, hidden_grad, proj_in, proj_out, val_features):
    tok, width = tokens.shape
    top = routes.shape[1]
    rank = proj_in.shape[1]
    groups = lax.axis_size("expert")
    dp = lax.axis_size("dp")
    exp_local, rows, hidden = hidden_grad.shape
    vals = val_features.shape[0]
    entries = rank * rank
    experts = exp_local * groups
    chunks = entries // LANES // dp

    val_split = val_features.reshape(vals, exp_local, dp, entries // dp).transpose(2, 0, 1, 3)
    val_all = lax.all_to_all(val_split, "dp", split_axis=0, concat_axis=0, tiled=True)

    pay_rows = rank + 2 * top + 8
    steps = 4
    pay = pl.pallas_call(
        act_kernel,
        out_shape=jax.ShapeDtypeStruct((pay_rows, tok), F32),
        grid=(steps,),
        in_specs=[
            pl.BlockSpec((tok, width // steps), lambda s: (0, s)),
            pl.BlockSpec((rank, width // steps), lambda s: (0, s)),
            pl.BlockSpec((top, tok), lambda s: (0, 0)),
            pl.BlockSpec((top, tok), lambda s: (0, 0)),
            pl.BlockSpec((1, tok), lambda s: (0, 0)),
        ],
        out_specs=pl.BlockSpec((pay_rows, tok), lambda s: (0, 0)),
        scratch_shapes=[pltpu.VMEM((rank, tok), F32)],
        cost_estimate=pl.CostEstimate(
            flops=2 * tok * width * rank, bytes_accessed=2 * width * (tok + rank), transcendentals=0
        ),
    )(tokens, proj_in.T, routes.T, gates.T, doc_ids.reshape(1, tok))

    pays = [pay]
    for k in range(1, groups):
        pays.append(lax.ppermute(pay, "expert", [(a, a ^ k) for a in range(groups)]))

    pair = 2
    low = pl.pallas_call(
        lowered_kernel,
        out_shape=jax.ShapeDtypeStruct((exp_local, rows, 2 * rank), BF16),
        grid=(exp_local // pair,),
        in_specs=[
            pl.BlockSpec((pair, rows, hidden), lambda s: (s, 0, 0)),
            pl.BlockSpec((pair, rank, hidden), lambda s: (s, 0, 0)),
        ],
        out_specs=pl.BlockSpec((pair, rows, 2 * rank), lambda s: (s, 0, 0)),
        cost_estimate=pl.CostEstimate(
            flops=2 * exp_local * rows * hidden * rank,
            bytes_accessed=2 * exp_local * hidden * (rows + rank),
            transcendentals=0,
        ),
    )(hidden_grad, proj_out.transpose(0, 2, 1))

    me = lax.axis_index("expert").astype(jnp.int32).reshape(1)
    vmem = pl.BlockSpec(memory_space=pltpu.VMEM)
    feats = pl.pallas_call(
        functools.partial(feature_kernel, groups, rank, top),
        out_shape=jax.ShapeDtypeStruct((dp, DOC_GRP, chunks, exp_local, LANES), BF16),
        in_specs=[pl.BlockSpec(memory_space=pltpu.SMEM)] + [vmem] * (groups + 1),
        out_specs=vmem,
        scratch_shapes=[
            pltpu.VMEM((exp_local, rows, 2 * rank), BF16),
            pltpu.VMEM((DOC_GRP * rank // 2 * exp_local, 2 * rank), F32),
        ],
    )(me, *pays, low)
    feats_all = lax.all_to_all(feats, "dp", split_axis=0, concat_axis=0, tiled=True)

    scale = 1.0 / float(experts * entries) ** 0.5
    part = pl.pallas_call(
        functools.partial(score_kernel, scale),
        out_shape=jax.ShapeDtypeStruct((groups * dp, DOC_GRP, dp * vals), F32),
        in_specs=[vmem, vmem],
        out_specs=vmem,
    )(feats_all, val_all)
    parts = lax.all_to_all(part, ("expert", "dp"), split_axis=0, concat_axis=0, tiled=True)
    return jnp.sum(parts, axis=0)


def solution(mesh):
    in_specs = (
        P(("expert", "dp"), None),
        P(("expert", "dp"), None),
        P(("expert", "dp"), None),
        P(("expert", "dp")),
        P("expert", "dp", None),
        P(),
        P("expert", None, None),
        P("dp", "expert", None),
    )
    out_specs = P("dp", None)
    return jax.shard_map(body, mesh=mesh, in_specs=in_specs, out_specs=out_specs, check_vma=False)
```

```python
import functools

import jax
import jax.numpy as jnp
from jax import lax
from jax.experimental import pallas as pl
from jax.experimental.pallas import tpu as pltpu
from jax.sharding import PartitionSpec as P


DOC_GRP = 2
LANES = 128
F32 = jnp.float32
BF16 = jnp.bfloat16
NT = (((1,), (1,)), ((), ()))
TN = (((0,), (0,)), ((), ()))


def act_kernel(tok_hbm, proj_hbm, routes_ref, gates_ref, docs_ref, out_ref, tok_ref, proj_ref, acc_ref, sems):
    rank = proj_ref.shape[0]
    top = routes_ref.shape[0]
    half = rank // 2
    steps = sems.shape[0]
    width = tok_ref.shape[1] // steps
    copies = []
    for s in range(steps):
        cols = pl.ds(s * width, width)
        copies.append(
            (
                pltpu.make_async_copy(proj_hbm.at[:, cols], proj_ref.at[:, cols], sems.at[s, 0]),
                pltpu.make_async_copy(tok_hbm.at[:, cols], tok_ref.at[:, cols], sems.at[s, 1]),
            )
        )
    for pair in copies:
        for copy in pair:
            copy.start()
    out_ref[rank : rank + top, :] = routes_ref[...].astype(F32)
    out_ref[rank + top : rank + 2 * top, :] = gates_ref[...]
    out_ref[rank + 2 * top :, :] = jnp.broadcast_to(
        docs_ref[...].astype(F32), (out_ref.shape[0] - rank - 2 * top, out_ref.shape[1])
    )
    total = jnp.zeros(acc_ref.shape, F32)
    for s in range(steps):
        for copy in copies[s]:
            copy.wait()
        cols = slice(s * width, (s + 1) * width)
        total += lax.dot_general(
            proj_ref[:, cols], tok_ref[:, cols], NT, preferred_element_type=F32
        )
    acc_ref[...] = total
    out_ref[0:half, :] = acc_ref[pl.ds(0, half, stride=2), :]
    out_ref[half:rank, :] = acc_ref[pl.ds(1, half, stride=2), :]


def lowered_kernel(grad_hbm, proj_hbm, out_ref, grad_ref, proj_ref, sems):
    copies = []
    for e in range(sems.shape[0]):
        copies.append(
            (
                pltpu.make_async_copy(proj_hbm.at[e], proj_ref.at[e], sems.at[e, 0]),
                pltpu.make_async_copy(grad_hbm.at[e], grad_ref.at[e], sems.at[e, 1]),
            )
        )
    for pair in copies:
        for copy in pair:
            copy.start()
    for e in range(sems.shape[0]):
        for copy in copies[e]:
            copy.wait()
        low = lax.dot_general(grad_ref[e], proj_ref[e], NT, preferred_element_type=F32)
        out_ref[e] = jnp.concatenate([low, low], axis=1).astype(BF16)


def feature_kernel(groups, rank, top, me_ref, *refs):
    pays, low_ref, out_ref, a_ref, f_ref = refs[:groups], *refs[groups:]
    exp_local, rows, _ = low_ref.shape
    cap = rows // groups
    tok = pays[0].shape[1]
    half = rank // 2
    me = me_ref[0]
    base = (me * exp_local).astype(F32)
    experts = lax.broadcasted_iota(jnp.int32, (exp_local, tok), 0).astype(F32) + base
    before = (
        lax.broadcasted_iota(jnp.int32, (tok, tok), 0)
        < lax.broadcasted_iota(jnp.int32, (tok, tok), 1)
    ).astype(BF16)
    slots = lax.broadcasted_iota(jnp.int32, (cap, tok), 0).astype(F32)
    for k in range(groups):
        pay = pays[k]
        hit = jnp.zeros((exp_local, tok), F32)
        gate = jnp.zeros((exp_local, tok), F32)
        for t in range(top):
            same = pay[rank + t : rank + t + 1, :] == experts
            hit = jnp.where(same, 1.0, hit)
            gate = jnp.where(same, pay[rank + top + t : rank + top + t + 1, :], gate)
        slot = jnp.dot(hit.astype(BF16), before, preferred_element_type=F32)
        slot = jnp.where(hit > 0.0, slot, -1.0)
        doc = pay[rank + 2 * top : rank + 2 * top + 1, :]
        parts = []
        for par in range(2):
            act = pay[par * half : (par + 1) * half, :]
            for d in range(DOC_GRP):
                parts.append(jnp.where(doc == float(d), act, 0.0))
        act = jnp.concatenate(parts, axis=0)
        high = act.astype(BF16)
        low = (act - high.astype(F32)).astype(BF16)
        right = jnp.concatenate([high, low], axis=1)
        picks, scales = [], []
        for e in range(exp_local):
            pick = slot[e : e + 1, :] == slots
            picks.append(jnp.where(pick, 1.0, 0.0).astype(BF16))
            scales.append(
                jnp.sum(jnp.where(pick, gate[e : e + 1, :], 0.0), axis=1, keepdims=True)
            )
        left = jnp.concatenate(picks, axis=0)
        scale = jnp.concatenate(scales, axis=0)
        left = jnp.concatenate([left, left], axis=1)
        sent = lax.dot_general(left, right, NT, preferred_element_type=F32) * scale
        sent = sent.astype(BF16)
        source = pl.multiple_of(lax.bitwise_xor(me, k) * cap, cap)
        for e in range(exp_local):
            a_ref[e, pl.ds(source, cap), :] = sent[e * cap : (e + 1) * cap, :]
    wide = DOC_GRP * half
    lane = lax.broadcasted_iota(jnp.int32, (wide, 2 * rank), 1)
    for e in range(exp_local):
        feat = lax.dot_general(a_ref[e], low_ref[e], TN, preferred_element_type=F32)
        f_ref[pl.ds(e, wide, stride=exp_local), :] = jnp.where(
            lane < rank, feat[:wide], feat[wide:]
        )
    parts, _, chunks, _, _ = out_ref.shape
    size = chunks * exp_local
    for d in range(DOC_GRP):
        for p in range(parts):
            start = (d * half + p * chunks) * exp_local
            out_ref[p, d] = (
                f_ref[start : start + size, :].astype(BF16).reshape(chunks, exp_local, 2 * rank)
            )


def score_kernel(scale, feat_ref, val_ref, out_ref):
    dp, docs, chunks, exp_local, lanes = feat_ref.shape
    vals = val_ref.shape[1]
    left_rows, right_rows = dp * docs * exp_local, dp * vals * exp_local
    total = jnp.zeros((left_rows, right_rows), F32)
    for c in range(chunks):
        left = feat_ref[:, :, c].reshape(left_rows, lanes)
        right = val_ref[:, :, :, c * lanes : (c + 1) * lanes].reshape(right_rows, lanes)
        total += lax.dot_general(left, right, NT, preferred_element_type=F32)
    row = lax.broadcasted_iota(jnp.int32, total.shape, 0) % exp_local
    col = lax.broadcasted_iota(jnp.int32, total.shape, 1) % exp_local
    total = jnp.where(row == col, total, 0.0)
    total = jnp.sum(total.reshape(dp * docs, exp_local, right_rows), axis=1)
    pick = (
        lax.broadcasted_iota(jnp.int32, (right_rows, dp * vals), 0) // exp_local
        == lax.broadcasted_iota(jnp.int32, (right_rows, dp * vals), 1)
    ).astype(F32)
    scores = jnp.dot(
        total, pick, preferred_element_type=F32, precision=lax.Precision.HIGHEST
    ) * scale
    for i in range(out_ref.shape[0] // dp):
        for j in range(dp):
            out_ref[i * dp + j] = scores[j * docs : (j + 1) * docs, :]


def layer(tokens, gates, routes, doc_ids, hidden_grad, proj_in, proj_out, val_features):
    tok, width = tokens.shape
    top = routes.shape[1]
    rank = proj_in.shape[1]
    groups = lax.axis_size("expert")
    dp = lax.axis_size("dp")
    exp_local, rows, hidden = hidden_grad.shape
    vals = val_features.shape[0]
    entries = rank * rank
    experts = exp_local * groups
    chunks = entries // LANES // dp

    val_split = val_features.reshape(vals, exp_local, dp, entries // dp).transpose(2, 0, 1, 3)
    val_all = lax.all_to_all(val_split, "dp", split_axis=0, concat_axis=0, tiled=True)

    vmem = pl.BlockSpec(memory_space=pltpu.VMEM)
    hbm = pl.BlockSpec(memory_space=pltpu.HBM)
    pay_rows = rank + 2 * top + 8
    steps = 4
    pay = pl.pallas_call(
        act_kernel,
        out_shape=jax.ShapeDtypeStruct((pay_rows, tok), F32),
        in_specs=[hbm, hbm, vmem, vmem, vmem],
        out_specs=vmem,
        scratch_shapes=[
            pltpu.VMEM((tok, width), BF16),
            pltpu.VMEM((rank, width), BF16),
            pltpu.VMEM((rank, tok), F32),
            pltpu.SemaphoreType.DMA((steps, 2)),
        ],
        compiler_params=pltpu.CompilerParams(vmem_limit_bytes=63 << 20),
        cost_estimate=pl.CostEstimate(
            flops=2 * tok * width * rank,
            bytes_accessed=2 * width * (tok + rank),
            transcendentals=0,
        ),
    )(tokens, proj_in.T, routes.T, gates.T, doc_ids.reshape(1, tok))

    pays = [pay]
    for k in range(1, groups):
        pays.append(lax.ppermute(pay, "expert", [(a, a ^ k) for a in range(groups)]))

    low = pl.pallas_call(
        lowered_kernel,
        out_shape=jax.ShapeDtypeStruct((exp_local, rows, 2 * rank), BF16),
        in_specs=[hbm, hbm],
        out_specs=vmem,
        scratch_shapes=[
            pltpu.VMEM((exp_local, rows, hidden), BF16),
            pltpu.VMEM((exp_local, rank, hidden), BF16),
            pltpu.SemaphoreType.DMA((exp_local, 2)),
        ],
        compiler_params=pltpu.CompilerParams(vmem_limit_bytes=62 << 20),
        cost_estimate=pl.CostEstimate(
            flops=2 * exp_local * rows * hidden * rank,
            bytes_accessed=2 * exp_local * hidden * (rows + rank),
            transcendentals=0,
        ),
    )(hidden_grad, proj_out.transpose(0, 2, 1))

    me = lax.axis_index("expert").astype(jnp.int32).reshape(1)
    feats = pl.pallas_call(
        functools.partial(feature_kernel, groups, rank, top),
        out_shape=jax.ShapeDtypeStruct((dp, DOC_GRP, chunks, exp_local, LANES), BF16),
        in_specs=[pl.BlockSpec(memory_space=pltpu.SMEM)] + [vmem] * (groups + 1),
        out_specs=vmem,
        scratch_shapes=[
            pltpu.VMEM((exp_local, rows, 2 * rank), BF16),
            pltpu.VMEM((DOC_GRP * rank // 2 * exp_local, 2 * rank), F32),
        ],
        compiler_params=pltpu.CompilerParams(vmem_limit_bytes=16 << 20),
    )(me, *pays, low)
    feats_all = lax.all_to_all(feats, "dp", split_axis=0, concat_axis=0, tiled=True)

    scale = 1.0 / float(experts * entries) ** 0.5
    part = pl.pallas_call(
        functools.partial(score_kernel, scale),
        out_shape=jax.ShapeDtypeStruct((groups * dp, DOC_GRP, dp * vals), F32),
        in_specs=[vmem, vmem],
        out_specs=vmem,
        compiler_params=pltpu.CompilerParams(vmem_limit_bytes=40 << 20),
    )(feats_all, val_all)
    parts = lax.all_to_all(part, ("expert", "dp"), split_axis=0, concat_axis=0, tiled=True)
    return jnp.sum(parts, axis=0)


def solution(mesh):
    in_specs = (
        P(("expert", "dp"), None),
        P(("expert", "dp"), None),
        P(("expert", "dp"), None),
        P(("expert", "dp")),
        P("expert", "dp", None),
        P(),
        P("expert", None, None),
        P("dp", "expert", None),
    )
    out_specs = P("dp", None)
    return jax.shard_map(layer, mesh=mesh, in_specs=in_specs, out_specs=out_specs, check_vma=False)
```

```python
import functools

import jax
import jax.numpy as jnp
from jax import lax
from jax.experimental import pallas as pl
from jax.experimental.pallas import tpu as pltpu
from jax.sharding import PartitionSpec as P


DOC_GRP = 2
LANES = 128
VL_F = 53 << 20
F32 = jnp.float32
BF16 = jnp.bfloat16
NT = (((1,), (1,)), ((), ()))
TN = (((0,), (0,)), ((), ()))


def act_kernel(
    tok_hbm, proj_hbm, val_hbm, routes_ref, gates_ref, docs_ref, out_ref, split_ref, *scratch
):
    tok_ref, proj_ref, acc_ref, sems, split_sems = scratch
    rank = proj_ref.shape[0]
    top = routes_ref.shape[0]
    half = rank // 2
    steps = sems.shape[0]
    width = tok_ref.shape[1] // steps
    copies = []
    for s in range(steps):
        cols = pl.ds(s * width, width)
        copies.append(
            (
                pltpu.make_async_copy(proj_hbm.at[:, cols], proj_ref.at[:, cols], sems.at[s, 0]),
                pltpu.make_async_copy(tok_hbm.at[:, cols], tok_ref.at[:, cols], sems.at[s, 1]),
            )
        )
    for pair in copies:
        for copy in pair:
            copy.start()
    parts, _, _, piece = split_ref.shape
    splits = [
        pltpu.make_async_copy(
            val_hbm.at[:, :, pl.ds(j * piece, piece)], split_ref.at[j], split_sems.at[j]
        )
        for j in range(parts)
    ]
    for copy in splits:
        copy.start()
    out_ref[rank : rank + top, :] = routes_ref[...].astype(F32)
    out_ref[rank + top : rank + 2 * top, :] = gates_ref[...]
    out_ref[rank + 2 * top :, :] = jnp.broadcast_to(
        docs_ref[...].astype(F32), (out_ref.shape[0] - rank - 2 * top, out_ref.shape[1])
    )
    total = jnp.zeros(acc_ref.shape, F32)
    for s in range(steps):
        for copy in copies[s]:
            copy.wait()
        cols = slice(s * width, (s + 1) * width)
        total += lax.dot_general(
            proj_ref[:, cols], tok_ref[:, cols], NT, preferred_element_type=F32
        )
    acc_ref[...] = total
    out_ref[0:half, :] = acc_ref[pl.ds(0, half, stride=2), :]
    out_ref[half:rank, :] = acc_ref[pl.ds(1, half, stride=2), :]
    for copy in splits:
        copy.wait()


def feature_kernel(groups, rank, top, me_ref, *refs):
    pays = refs[:groups]
    grad_hbm, proj_hbm, out_ref, a_ref, f_ref, grad_ref, proj_ref, sems = refs[groups:]
    exp_local, rows, _ = grad_ref.shape
    batch = exp_local // sems.shape[0]
    copies = []
    for n in range(sems.shape[0]):
        part = pl.ds(n * batch, batch)
        copies.append(
            (
                pltpu.make_async_copy(proj_hbm.at[part], proj_ref.at[part], sems.at[n, 0]),
                pltpu.make_async_copy(grad_hbm.at[part], grad_ref.at[part], sems.at[n, 1]),
            )
        )
    for pair in copies:
        for copy in pair:
            copy.start()
    cap = rows // groups
    tok = pays[0].shape[1]
    half = rank // 2
    me = me_ref[0]
    base = (me * exp_local).astype(F32)
    experts = lax.broadcasted_iota(jnp.int32, (exp_local, tok), 0).astype(F32) + base
    before = (
        lax.broadcasted_iota(jnp.int32, (tok, tok), 0)
        < lax.broadcasted_iota(jnp.int32, (tok, tok), 1)
    ).astype(BF16)
    slots = lax.broadcasted_iota(jnp.int32, (cap, tok), 0).astype(F32)
    for k in range(groups):
        pay = pays[k]
        hit = jnp.zeros((exp_local, tok), F32)
        gate = jnp.zeros((exp_local, tok), F32)
        for t in range(top):
            same = pay[rank + t : rank + t + 1, :] == experts
            hit = jnp.where(same, 1.0, hit)
            gate = jnp.where(same, pay[rank + top + t : rank + top + t + 1, :], gate)
        slot = jnp.dot(hit.astype(BF16), before, preferred_element_type=F32)
        slot = jnp.where(hit > 0.0, slot, -1.0)
        doc = pay[rank + 2 * top : rank + 2 * top + 1, :]
        parts = []
        for par in range(2):
            act = pay[par * half : (par + 1) * half, :]
            for d in range(DOC_GRP):
                parts.append(jnp.where(doc == float(d), act, 0.0))
        act = jnp.concatenate(parts, axis=0)
        high = act.astype(BF16)
        low = (act - high.astype(F32)).astype(BF16)
        right = jnp.concatenate([high, low], axis=1)
        picks, scales = [], []
        for e in range(exp_local):
            pick = slot[e : e + 1, :] == slots
            picks.append(jnp.where(pick, 1.0, 0.0).astype(BF16))
            scales.append(
                jnp.sum(jnp.where(pick, gate[e : e + 1, :], 0.0), axis=1, keepdims=True)
            )
        left = jnp.concatenate(picks, axis=0)
        scale = jnp.concatenate(scales, axis=0)
        left = jnp.concatenate([left, left], axis=1)
        sent = lax.dot_general(left, right, NT, preferred_element_type=F32) * scale
        sent = sent.astype(BF16)
        source = pl.multiple_of(lax.bitwise_xor(me, k) * cap, cap)
        for e in range(exp_local):
            a_ref[e, pl.ds(source, cap), :] = sent[e * cap : (e + 1) * cap, :]
    wide = DOC_GRP * half
    lane = lax.broadcasted_iota(jnp.int32, (wide, 2 * rank), 1)
    for e in range(exp_local):
        if e % batch == 0:
            for copy in copies[e // batch]:
                copy.wait()
        low = lax.dot_general(grad_ref[e], proj_ref[e], NT, preferred_element_type=F32)
        low = jnp.concatenate([low, low], axis=1).astype(BF16)
        feat = lax.dot_general(a_ref[e], low, TN, preferred_element_type=F32)
        f_ref[pl.ds(e, wide, stride=exp_local), :] = jnp.where(
            lane < rank, feat[:wide], feat[wide:]
        )
    parts, _, chunks, _, _ = out_ref.shape
    size = chunks * exp_local
    for d in range(DOC_GRP):
        for p in range(parts):
            start = (d * half + p * chunks) * exp_local
            out_ref[p, d] = (
                f_ref[start : start + size, :].astype(BF16).reshape(chunks, exp_local, 2 * rank)
            )


def score_kernel(scale, feat_ref, val_ref, out_ref):
    dp, docs, chunks, exp_local, lanes = feat_ref.shape
    vals = val_ref.shape[1]
    left_rows, right_rows = dp * docs * exp_local, dp * vals * exp_local
    total = jnp.zeros((left_rows, right_rows), F32)
    for c in range(chunks):
        left = feat_ref[:, :, c].reshape(left_rows, lanes)
        right = val_ref[:, :, :, c * lanes : (c + 1) * lanes].reshape(right_rows, lanes)
        total += lax.dot_general(left, right, NT, preferred_element_type=F32)
    row = lax.broadcasted_iota(jnp.int32, total.shape, 0) % exp_local
    col = lax.broadcasted_iota(jnp.int32, total.shape, 1) % exp_local
    total = jnp.where(row == col, total, 0.0)
    total = jnp.sum(total.reshape(dp * docs, exp_local, right_rows), axis=1)
    pick = (
        lax.broadcasted_iota(jnp.int32, (right_rows, dp * vals), 0) // exp_local
        == lax.broadcasted_iota(jnp.int32, (right_rows, dp * vals), 1)
    ).astype(F32)
    scores = jnp.dot(
        total, pick, preferred_element_type=F32, precision=lax.Precision.HIGHEST
    ) * scale
    for i in range(out_ref.shape[0] // dp):
        for j in range(dp):
            out_ref[i * dp + j] = scores[j * docs : (j + 1) * docs, :]


def layer(tokens, gates, routes, doc_ids, hidden_grad, proj_in, proj_out, val_features):
    tok, width = tokens.shape
    top = routes.shape[1]
    rank = proj_in.shape[1]
    groups = lax.axis_size("expert")
    dp = lax.axis_size("dp")
    exp_local, rows, hidden = hidden_grad.shape
    vals = val_features.shape[0]
    entries = rank * rank
    experts = exp_local * groups
    chunks = entries // LANES // dp

    vmem = pl.BlockSpec(memory_space=pltpu.VMEM)
    hbm = pl.BlockSpec(memory_space=pltpu.HBM)
    pay_rows = rank + 2 * top + 8
    steps = 2
    pay, val_split = pl.pallas_call(
        act_kernel,
        out_shape=(
            jax.ShapeDtypeStruct((pay_rows, tok), F32),
            jax.ShapeDtypeStruct((dp, vals, exp_local, entries // dp), BF16),
        ),
        in_specs=[hbm, hbm, hbm, vmem, vmem, vmem],
        out_specs=(vmem, vmem),
        scratch_shapes=[
            pltpu.VMEM((tok, width), BF16),
            pltpu.VMEM((rank, width), BF16),
            pltpu.VMEM((rank, tok), F32),
            pltpu.SemaphoreType.DMA((steps, 2)),
            pltpu.SemaphoreType.DMA((dp,)),
        ],
        compiler_params=pltpu.CompilerParams(vmem_limit_bytes=63 << 20),
        cost_estimate=pl.CostEstimate(
            flops=2 * tok * width * rank,
            bytes_accessed=2 * width * (tok + rank),
            transcendentals=0,
        ),
    )(tokens, proj_in.T, val_features, routes.T, gates.T, doc_ids.reshape(1, tok))

    val_all = lax.all_to_all(val_split, "dp", split_axis=0, concat_axis=0, tiled=True)

    pays = [pay]
    for k in range(1, groups):
        pays.append(lax.ppermute(pay, "expert", [(a, a ^ k) for a in range(groups)]))

    me = lax.axis_index("expert").astype(jnp.int32).reshape(1)
    feats = pl.pallas_call(
        functools.partial(feature_kernel, groups, rank, top),
        out_shape=jax.ShapeDtypeStruct((dp, DOC_GRP, chunks, exp_local, LANES), BF16),
        in_specs=[pl.BlockSpec(memory_space=pltpu.SMEM)] + [vmem] * groups + [hbm, hbm],
        out_specs=vmem,
        scratch_shapes=[
            pltpu.VMEM((exp_local, rows, 2 * rank), BF16),
            pltpu.VMEM((DOC_GRP * rank // 2 * exp_local, 2 * rank), F32),
            pltpu.VMEM((exp_local, rows, hidden), BF16),
            pltpu.VMEM((exp_local, rank, hidden), BF16),
            pltpu.SemaphoreType.DMA((4, 2)),
        ],
        compiler_params=pltpu.CompilerParams(vmem_limit_bytes=VL_F),
        cost_estimate=pl.CostEstimate(
            flops=2 * exp_local * rows * hidden * rank,
            bytes_accessed=2 * exp_local * hidden * (rows + rank),
            transcendentals=0,
        ),
    )(me, *pays, hidden_grad, proj_out.transpose(0, 2, 1))
    feats_all = lax.all_to_all(feats, "dp", split_axis=0, concat_axis=0, tiled=True)

    scale = 1.0 / float(experts * entries) ** 0.5
    part = pl.pallas_call(
        functools.partial(score_kernel, scale),
        out_shape=jax.ShapeDtypeStruct((groups * dp, DOC_GRP, dp * vals), F32),
        in_specs=[vmem, vmem],
        out_specs=vmem,
        compiler_params=pltpu.CompilerParams(vmem_limit_bytes=40 << 20),
    )(feats_all, val_all)
    parts = lax.all_to_all(part, ("expert", "dp"), split_axis=0, concat_axis=0, tiled=True)
    return jnp.sum(parts, axis=0)


def solution(mesh):
    in_specs = (
        P(("expert", "dp"), None),
        P(("expert", "dp"), None),
        P(("expert", "dp"), None),
        P(("expert", "dp")),
        P("expert", "dp", None),
        P(),
        P("expert", None, None),
        P("dp", "expert", None),
    )
    out_specs = P("dp", None)
    return jax.shard_map(layer, mesh=mesh, in_specs=in_specs, out_specs=out_specs, check_vma=False)
```

```python
import functools

import jax
import jax.numpy as jnp
from jax import lax
from jax.experimental import pallas as pl
from jax.experimental.pallas import tpu as pltpu
from jax.sharding import PartitionSpec as P


DOC_GRP = 2
LANES = 128
VL_F = 53 << 20
F32 = jnp.float32
BF16 = jnp.bfloat16
NT = (((1,), (1,)), ((), ()))
TN = (((0,), (0,)), ((), ()))


def act_kernel(
    tok_hbm, proj_hbm, val_hbm, routes_ref, gates_ref, docs_ref, out_ref, split_ref, *scratch
):
    tok_ref, proj_ref, acc_ref, piece_ref, sems, split_sems = scratch
    rank = proj_ref.shape[0]
    top = routes_ref.shape[0]
    half = rank // 2
    steps = sems.shape[0]
    width = tok_ref.shape[1] // steps
    copies = []
    for s in range(steps):
        cols = pl.ds(s * width, width)
        copies.append(
            (
                pltpu.make_async_copy(proj_hbm.at[:, cols], proj_ref.at[:, cols], sems.at[s, 0]),
                pltpu.make_async_copy(tok_hbm.at[:, cols], tok_ref.at[:, cols], sems.at[s, 1]),
            )
        )
    parts, _, _, piece = piece_ref.shape
    splits = [
        pltpu.make_async_copy(
            val_hbm.at[:, :, pl.ds(j * piece, piece)], piece_ref.at[j], split_sems.at[j]
        )
        for j in range(parts)
    ]
    whole = pltpu.make_async_copy(piece_ref, split_ref, split_sems.at[parts])
    for copy in splits:
        copy.start()
    for pair in copies:
        for copy in pair:
            copy.start()
    out_ref[rank : rank + top, :] = routes_ref[...].astype(F32)
    out_ref[rank + top : rank + 2 * top, :] = gates_ref[...]
    out_ref[rank + 2 * top :, :] = jnp.broadcast_to(
        docs_ref[...].astype(F32), (out_ref.shape[0] - rank - 2 * top, out_ref.shape[1])
    )
    for copy in splits:
        copy.wait()
    whole.start()
    total = jnp.zeros(acc_ref.shape, F32)
    for s in range(steps):
        for copy in copies[s]:
            copy.wait()
        cols = slice(s * width, (s + 1) * width)
        total += lax.dot_general(
            proj_ref[:, cols], tok_ref[:, cols], NT, preferred_element_type=F32
        )
    acc_ref[...] = total
    out_ref[0:half, :] = acc_ref[pl.ds(0, half, stride=2), :]
    out_ref[half:rank, :] = acc_ref[pl.ds(1, half, stride=2), :]
    whole.wait()


def feature_kernel(groups, parts, rank, top, me_ref, *refs):
    pays = refs[:groups]
    grad_hbm, proj_hbm = refs[groups : groups + 2]
    outs = refs[groups + 2 : groups + 2 + parts]
    a_ref, low_ref, f_ref, grad_ref, proj_ref, sems = refs[groups + 2 + parts :]
    exp_local, rows, _ = grad_ref.shape
    batch = exp_local // sems.shape[0]
    copies = []
    for n in range(sems.shape[0]):
        part = pl.ds(n * batch, batch)
        copies.append(
            (
                pltpu.make_async_copy(proj_hbm.at[part], proj_ref.at[part], sems.at[n, 0]),
                pltpu.make_async_copy(grad_hbm.at[part], grad_ref.at[part], sems.at[n, 1]),
            )
        )
    for pair in copies:
        for copy in pair:
            copy.start()
    cap = rows // groups
    tok = pays[0].shape[1]
    half = rank // 2
    me = me_ref[0]
    base = (me * exp_local).astype(F32)
    experts = lax.broadcasted_iota(jnp.int32, (exp_local, tok), 0).astype(F32) + base
    before = (
        lax.broadcasted_iota(jnp.int32, (tok, tok), 0)
        < lax.broadcasted_iota(jnp.int32, (tok, tok), 1)
    ).astype(BF16)
    slots = lax.broadcasted_iota(jnp.int32, (cap, tok), 0).astype(F32)
    for k in range(groups):
        pay = pays[k]
        hit = jnp.zeros((exp_local, tok), F32)
        gate = jnp.zeros((exp_local, tok), F32)
        for t in range(top):
            same = pay[rank + t : rank + t + 1, :] == experts
            hit = jnp.where(same, 1.0, hit)
            gate = jnp.where(same, pay[rank + top + t : rank + top + t + 1, :], gate)
        slot = jnp.dot(hit.astype(BF16), before, preferred_element_type=F32)
        slot = jnp.where(hit > 0.0, slot, -1.0)
        doc = pay[rank + 2 * top : rank + 2 * top + 1, :]
        masked = []
        for par in range(2):
            act = pay[par * half : (par + 1) * half, :]
            for d in range(DOC_GRP):
                masked.append(jnp.where(doc == float(d), act, 0.0))
        act = jnp.concatenate(masked, axis=0)
        high = act.astype(BF16)
        low = (act - high.astype(F32)).astype(BF16)
        right = jnp.concatenate([high, low], axis=1)
        picks, scales = [], []
        for e in range(exp_local):
            pick = slot[e : e + 1, :] == slots
            picks.append(jnp.where(pick, 1.0, 0.0).astype(BF16))
            scales.append(
                jnp.sum(jnp.where(pick, gate[e : e + 1, :], 0.0), axis=1, keepdims=True)
            )
        left = jnp.concatenate(picks, axis=0)
        scale = jnp.concatenate(scales, axis=0)
        left = jnp.concatenate([left, left], axis=1)
        sent = lax.dot_general(left, right, NT, preferred_element_type=F32) * scale
        sent = sent.astype(BF16)
        source = pl.multiple_of(lax.bitwise_xor(me, k) * cap, cap)
        for e in range(exp_local):
            a_ref[e, pl.ds(source, cap), :] = sent[e * cap : (e + 1) * cap, :]
    wide = DOC_GRP * half
    lane = lax.broadcasted_iota(jnp.int32, (wide, 2 * rank), 1)

    def project(n):
        for copy in copies[n]:
            copy.wait()
        for e in range(n * batch, (n + 1) * batch):
            low = lax.dot_general(grad_ref[e], proj_ref[e], NT, preferred_element_type=F32)
            low_ref[e] = jnp.concatenate([low, low], axis=1).astype(BF16)

    def outer(n):
        for e in range(n * batch, (n + 1) * batch):
            feat = lax.dot_general(a_ref[e], low_ref[e], TN, preferred_element_type=F32)
            f_ref[pl.ds(e, wide, stride=exp_local), :] = jnp.where(
                lane < rank, feat[:wide], feat[wide:]
            )

    for n in range(sems.shape[0]):
        project(n)
        if n:
            outer(n - 1)
    outer(sems.shape[0] - 1)
    _, chunks, _, _ = outs[0].shape
    size = chunks * exp_local
    for k in range(parts):
        part = lax.bitwise_xor(me_ref[1], k)
        for d in range(DOC_GRP):
            start = pl.multiple_of((d * half + part * chunks) * exp_local, size)
            outs[k][d] = (
                f_ref[pl.ds(start, size), :].astype(BF16).reshape(chunks, exp_local, 2 * rank)
            )


def score_kernel(parts, scale, me_ref, *refs):
    feats, val_ref, out_ref = refs[:parts], refs[parts], refs[parts + 1]
    docs, chunks, exp_local, lanes = feats[0].shape
    vals = val_ref.shape[1]
    left_rows, right_rows = parts * docs * exp_local, parts * vals * exp_local
    total = jnp.zeros((left_rows, right_rows), F32)
    for c in range(chunks):
        left = jnp.concatenate(
            [feat[:, c].reshape(docs * exp_local, lanes) for feat in feats], axis=0
        )
        right = val_ref[:, :, :, c * lanes : (c + 1) * lanes].reshape(right_rows, lanes)
        total += lax.dot_general(left, right, NT, preferred_element_type=F32)
    row = lax.broadcasted_iota(jnp.int32, total.shape, 0) % exp_local
    col = lax.broadcasted_iota(jnp.int32, total.shape, 1) % exp_local
    total = jnp.where(row == col, total, 0.0)
    total = jnp.sum(total.reshape(parts * docs, exp_local, right_rows), axis=1)
    pick = (
        lax.broadcasted_iota(jnp.int32, (right_rows, parts * vals), 0) // exp_local
        == lax.broadcasted_iota(jnp.int32, (right_rows, parts * vals), 1)
    ).astype(F32)
    scores = jnp.dot(
        total, pick, preferred_element_type=F32, precision=lax.Precision.HIGHEST
    ) * scale
    for k in range(parts):
        group = lax.bitwise_xor(me_ref[1], k)
        for i in range(out_ref.shape[0] // parts):
            out_ref[i * parts + group] = scores[k * docs : (k + 1) * docs, :]


def layer(tokens, gates, routes, doc_ids, hidden_grad, proj_in, proj_out, val_features):
    tok, width = tokens.shape
    top = routes.shape[1]
    rank = proj_in.shape[1]
    groups = lax.axis_size("expert")
    dp = lax.axis_size("dp")
    exp_local, rows, hidden = hidden_grad.shape
    vals = val_features.shape[0]
    entries = rank * rank
    experts = exp_local * groups
    chunks = entries // LANES // dp

    vmem = pl.BlockSpec(memory_space=pltpu.VMEM)
    hbm = pl.BlockSpec(memory_space=pltpu.HBM)
    pay_rows = rank + 2 * top + 8
    steps = 2
    pay, val_split = pl.pallas_call(
        act_kernel,
        out_shape=(
            jax.ShapeDtypeStruct((pay_rows, tok), F32),
            jax.ShapeDtypeStruct((dp, vals, exp_local, entries // dp), BF16),
        ),
        in_specs=[hbm, hbm, hbm, vmem, vmem, vmem],
        out_specs=(vmem, hbm),
        scratch_shapes=[
            pltpu.VMEM((tok, width), BF16),
            pltpu.VMEM((rank, width), BF16),
            pltpu.VMEM((rank, tok), F32),
            pltpu.VMEM((dp, vals, exp_local, entries // dp), BF16),
            pltpu.SemaphoreType.DMA((steps, 2)),
            pltpu.SemaphoreType.DMA((dp + 1,)),
        ],
        compiler_params=pltpu.CompilerParams(vmem_limit_bytes=63 << 20),
        cost_estimate=pl.CostEstimate(
            flops=2 * tok * width * rank,
            bytes_accessed=2 * width * (tok + rank),
            transcendentals=0,
        ),
    )(tokens, proj_in.T, val_features, routes.T, gates.T, doc_ids.reshape(1, tok))

    val_all = lax.all_to_all(val_split, "dp", split_axis=0, concat_axis=0, tiled=True)

    pays = [pay]
    for k in range(1, groups):
        pays.append(lax.ppermute(pay, "expert", [(a, a ^ k) for a in range(groups)]))

    me = jnp.stack([lax.axis_index("expert"), lax.axis_index("dp")]).astype(jnp.int32)
    smem = pl.BlockSpec(memory_space=pltpu.SMEM)
    block = jax.ShapeDtypeStruct((DOC_GRP, chunks, exp_local, LANES), BF16)
    feats = pl.pallas_call(
        functools.partial(feature_kernel, groups, dp, rank, top),
        out_shape=(block,) * dp,
        in_specs=[smem] + [vmem] * groups + [hbm, hbm],
        out_specs=(vmem,) * dp,
        scratch_shapes=[
            pltpu.VMEM((exp_local, rows, 2 * rank), BF16),
            pltpu.VMEM((exp_local, rows, 2 * rank), BF16),
            pltpu.VMEM((DOC_GRP * rank // 2 * exp_local, 2 * rank), F32),
            pltpu.VMEM((exp_local, rows, hidden), BF16),
            pltpu.VMEM((exp_local, rank, hidden), BF16),
            pltpu.SemaphoreType.DMA((4, 2)),
        ],
        compiler_params=pltpu.CompilerParams(vmem_limit_bytes=VL_F),
        cost_estimate=pl.CostEstimate(
            flops=2 * exp_local * rows * hidden * rank,
            bytes_accessed=2 * exp_local * hidden * (rows + rank),
            transcendentals=0,
        ),
    )(me, *pays, hidden_grad, proj_out.transpose(0, 2, 1))
    arrived = [feats[0]]
    for k in range(1, dp):
        arrived.append(lax.ppermute(feats[k], "dp", [(a, a ^ k) for a in range(dp)]))

    scale = 1.0 / float(experts * entries) ** 0.5
    part = pl.pallas_call(
        functools.partial(score_kernel, dp, scale),
        out_shape=jax.ShapeDtypeStruct((groups * dp, DOC_GRP, dp * vals), F32),
        in_specs=[smem] + [vmem] * (dp + 1),
        out_specs=vmem,
        compiler_params=pltpu.CompilerParams(vmem_limit_bytes=40 << 20),
    )(me, *arrived, val_all)
    parts = lax.all_to_all(part, ("expert", "dp"), split_axis=0, concat_axis=0, tiled=True)
    return jnp.sum(parts, axis=0)


def solution(mesh):
    in_specs = (
        P(("expert", "dp"), None),
        P(("expert", "dp"), None),
        P(("expert", "dp"), None),
        P(("expert", "dp")),
        P("expert", "dp", None),
        P(),
        P("expert", None, None),
        P("dp", "expert", None),
    )
    out_specs = P("dp", None)
    return jax.shard_map(layer, mesh=mesh, in_specs=in_specs, out_specs=out_specs, check_vma=False)
```

```python
import functools

import jax
import jax.numpy as jnp
from jax import lax
from jax.experimental import pallas as pl
from jax.experimental.pallas import tpu as pltpu
from jax.sharding import PartitionSpec as P


DOC_GRP = 2
LANES = 128
VL_S = 53 << 20
VL_A = 63 << 20
VL_L = 53 << 20
VL_F = 16 << 20
F32 = jnp.float32
BF16 = jnp.bfloat16
NT = (((1,), (1,)), ((), ()))
TN = (((0,), (0,)), ((), ()))


def split_kernel(val_hbm, out_ref, sems):
    parts, _, _, piece = out_ref.shape
    copies = [
        pltpu.make_async_copy(val_hbm.at[:, :, pl.ds(j * piece, piece)], out_ref.at[j], sems.at[j])
        for j in range(parts)
    ]
    for copy in copies:
        copy.start()
    for copy in copies:
        copy.wait()


def act_kernel(tok_hbm, proj_hbm, routes_hbm, gates_hbm, docs_hbm, out_ref, *scratch):
    tok_ref, proj_ref, routes_ref, gates_ref, docs_ref, acc_ref, sems, small_sems = scratch
    rank = proj_ref.shape[0]
    top = routes_ref.shape[0]
    half = rank // 2
    steps = sems.shape[0]
    width = tok_ref.shape[1] // steps
    copies = []
    for s in range(steps):
        cols = pl.ds(s * width, width)
        copies.append(
            (
                pltpu.make_async_copy(proj_hbm.at[:, cols], proj_ref.at[:, cols], sems.at[s, 0]),
                pltpu.make_async_copy(tok_hbm.at[:, cols], tok_ref.at[:, cols], sems.at[s, 1]),
            )
        )
    smalls = [
        pltpu.make_async_copy(routes_hbm, routes_ref, small_sems.at[0]),
        pltpu.make_async_copy(gates_hbm, gates_ref, small_sems.at[1]),
        pltpu.make_async_copy(docs_hbm, docs_ref, small_sems.at[2]),
    ]
    for copy in copies[0]:
        copy.start()
    for copy in smalls:
        copy.start()
    for pair in copies[1:]:
        for copy in pair:
            copy.start()
    for copy in smalls:
        copy.wait()
    out_ref[rank : rank + top, :] = routes_ref[...].astype(F32)
    out_ref[rank + top : rank + 2 * top, :] = gates_ref[...]
    out_ref[rank + 2 * top :, :] = jnp.broadcast_to(
        docs_ref[...].astype(F32), (out_ref.shape[0] - rank - 2 * top, out_ref.shape[1])
    )
    total = jnp.zeros(acc_ref.shape, F32)
    for s in range(steps):
        for copy in copies[s]:
            copy.wait()
        cols = slice(s * width, (s + 1) * width)
        total += lax.dot_general(
            proj_ref[:, cols], tok_ref[:, cols], NT, preferred_element_type=F32
        )
    acc_ref[...] = total
    out_ref[0:half, :] = acc_ref[pl.ds(0, half, stride=2), :]
    out_ref[half:rank, :] = acc_ref[pl.ds(1, half, stride=2), :]


def lowered_kernel(grad_hbm, proj_hbm, out_ref, grad_ref, proj_ref, sems):
    count = sems.shape[0]
    batch = grad_ref.shape[0] // count
    copies = []
    for n in range(count):
        part = pl.ds(n * batch, batch)
        copies.append(
            (
                pltpu.make_async_copy(proj_hbm.at[part], proj_ref.at[part], sems.at[n, 0]),
                pltpu.make_async_copy(grad_hbm.at[part], grad_ref.at[part], sems.at[n, 1]),
            )
        )
    for pair in copies:
        for copy in pair:
            copy.start()
    for n in range(count):
        for copy in copies[n]:
            copy.wait()
        for e in range(n * batch, (n + 1) * batch):
            low = lax.dot_general(grad_ref[e], proj_ref[e], NT, preferred_element_type=F32)
            out_ref[e] = jnp.concatenate([low, low], axis=1).astype(BF16)


def feature_kernel(groups, parts, rank, top, me_ref, *refs):
    pays = refs[:groups]
    low_ref = refs[groups]
    outs = refs[groups + 1 : groups + 1 + parts]
    a_ref, f_ref = refs[groups + 1 + parts :]
    exp_local, rows, _ = low_ref.shape
    cap = rows // groups
    tok = pays[0].shape[1]
    half = rank // 2
    me = me_ref[0]
    base = (me * exp_local).astype(F32)
    experts = lax.broadcasted_iota(jnp.int32, (exp_local, tok), 0).astype(F32) + base
    before = (
        lax.broadcasted_iota(jnp.int32, (tok, tok), 0)
        < lax.broadcasted_iota(jnp.int32, (tok, tok), 1)
    ).astype(BF16)
    slots = lax.broadcasted_iota(jnp.int32, (cap, tok), 0).astype(F32)
    for k in range(groups):
        pay = pays[k]
        hit = jnp.zeros((exp_local, tok), F32)
        gate = jnp.zeros((exp_local, tok), F32)
        for t in range(top):
            same = pay[rank + t : rank + t + 1, :] == experts
            hit = jnp.where(same, 1.0, hit)
            gate = jnp.where(same, pay[rank + top + t : rank + top + t + 1, :], gate)
        slot = jnp.dot(hit.astype(BF16), before, preferred_element_type=F32)
        slot = jnp.where(hit > 0.0, slot, -1.0)
        doc = pay[rank + 2 * top : rank + 2 * top + 1, :]
        masked = []
        for par in range(2):
            act = pay[par * half : (par + 1) * half, :]
            for d in range(DOC_GRP):
                masked.append(jnp.where(doc == float(d), act, 0.0))
        act = jnp.concatenate(masked, axis=0)
        high = act.astype(BF16)
        low = (act - high.astype(F32)).astype(BF16)
        right = jnp.concatenate([high, low], axis=1)
        picks, scales = [], []
        for e in range(exp_local):
            pick = slot[e : e + 1, :] == slots
            picks.append(jnp.where(pick, 1.0, 0.0).astype(BF16))
            scales.append(
                jnp.sum(jnp.where(pick, gate[e : e + 1, :], 0.0), axis=1, keepdims=True)
            )
        left = jnp.concatenate(picks, axis=0)
        scale = jnp.concatenate(scales, axis=0)
        left = jnp.concatenate([left, left], axis=1)
        sent = lax.dot_general(left, right, NT, preferred_element_type=F32) * scale
        sent = sent.astype(BF16)
        source = pl.multiple_of(lax.bitwise_xor(me, k) * cap, cap)
        for e in range(exp_local):
            a_ref[e, pl.ds(source, cap), :] = sent[e * cap : (e + 1) * cap, :]
    wide = DOC_GRP * half
    lane = lax.broadcasted_iota(jnp.int32, (wide, 2 * rank), 1)
    for e in range(exp_local):
        feat = lax.dot_general(a_ref[e], low_ref[e], TN, preferred_element_type=F32)
        f_ref[pl.ds(e, wide, stride=exp_local), :] = jnp.where(
            lane < rank, feat[:wide], feat[wide:]
        )
    _, chunks, _, _ = outs[0].shape
    size = chunks * exp_local
    for k in range(parts):
        part = lax.bitwise_xor(me_ref[1], k)
        for d in range(DOC_GRP):
            start = pl.multiple_of((d * half + part * chunks) * exp_local, size)
            outs[k][d] = (
                f_ref[pl.ds(start, size), :].astype(BF16).reshape(chunks, exp_local, 2 * rank)
            )


def score_kernel(parts, scale, me_ref, *refs):
    feats, val_ref, out_ref = refs[:parts], refs[parts], refs[parts + 1]
    docs, chunks, exp_local, lanes = feats[0].shape
    vals = val_ref.shape[1]
    left_rows, right_rows = parts * docs * exp_local, parts * vals * exp_local
    total = jnp.zeros((left_rows, right_rows), F32)
    for c in range(chunks):
        left = jnp.concatenate(
            [feat[:, c].reshape(docs * exp_local, lanes) for feat in feats], axis=0
        )
        right = val_ref[:, :, :, c * lanes : (c + 1) * lanes].reshape(right_rows, lanes)
        total += lax.dot_general(left, right, NT, preferred_element_type=F32)
    row = lax.broadcasted_iota(jnp.int32, total.shape, 0) % exp_local
    col = lax.broadcasted_iota(jnp.int32, total.shape, 1) % exp_local
    total = jnp.where(row == col, total, 0.0)
    total = jnp.sum(total.reshape(parts * docs, exp_local, right_rows), axis=1)
    pick = (
        lax.broadcasted_iota(jnp.int32, (right_rows, parts * vals), 0) // exp_local
        == lax.broadcasted_iota(jnp.int32, (right_rows, parts * vals), 1)
    ).astype(F32)
    scores = jnp.dot(
        total, pick, preferred_element_type=F32, precision=lax.Precision.HIGHEST
    ) * scale
    for k in range(parts):
        group = lax.bitwise_xor(me_ref[1], k)
        for i in range(out_ref.shape[0] // parts):
            out_ref[i * parts + group] = scores[k * docs : (k + 1) * docs, :]


def layer(tokens, gates, routes, doc_ids, hidden_grad, proj_in, proj_out, val_features):
    tok, width = tokens.shape
    top = routes.shape[1]
    rank = proj_in.shape[1]
    groups = lax.axis_size("expert")
    dp = lax.axis_size("dp")
    exp_local, rows, hidden = hidden_grad.shape
    vals = val_features.shape[0]
    entries = rank * rank
    experts = exp_local * groups
    chunks = entries // LANES // dp

    vmem = pl.BlockSpec(memory_space=pltpu.VMEM)
    hbm = pl.BlockSpec(memory_space=pltpu.HBM)
    val_split = pl.pallas_call(
        split_kernel,
        out_shape=jax.ShapeDtypeStruct((dp, vals, exp_local, entries // dp), BF16),
        in_specs=[hbm],
        out_specs=vmem,
        scratch_shapes=[pltpu.SemaphoreType.DMA((dp,))],
        compiler_params=pltpu.CompilerParams(vmem_limit_bytes=VL_S),
    )(val_features)
    val_all = lax.all_to_all(val_split, "dp", split_axis=0, concat_axis=0, tiled=True)

    pay_rows = rank + 2 * top + 8
    steps = 2
    pay = pl.pallas_call(
        act_kernel,
        out_shape=jax.ShapeDtypeStruct((pay_rows, tok), F32),
        in_specs=[hbm] * 5,
        out_specs=vmem,
        scratch_shapes=[
            pltpu.VMEM((tok, width), BF16),
            pltpu.VMEM((rank, width), BF16),
            pltpu.VMEM((top, tok), jnp.int32),
            pltpu.VMEM((top, tok), F32),
            pltpu.VMEM((1, tok), jnp.int32),
            pltpu.VMEM((rank, tok), F32),
            pltpu.SemaphoreType.DMA((steps, 2)),
            pltpu.SemaphoreType.DMA((3,)),
        ],
        compiler_params=pltpu.CompilerParams(vmem_limit_bytes=VL_A),
        cost_estimate=pl.CostEstimate(
            flops=2 * tok * width * rank,
            bytes_accessed=2 * width * (tok + rank),
            transcendentals=0,
        ),
    )(tokens, proj_in.T, routes.T, gates.T, doc_ids.reshape(1, tok))

    pays = [pay]
    for k in range(1, groups):
        pays.append(lax.ppermute(pay, "expert", [(a, a ^ k) for a in range(groups)]))

    low = pl.pallas_call(
        lowered_kernel,
        out_shape=jax.ShapeDtypeStruct((exp_local, rows, 2 * rank), BF16),
        in_specs=[hbm, hbm],
        out_specs=vmem,
        scratch_shapes=[
            pltpu.VMEM((exp_local, rows, hidden), BF16),
            pltpu.VMEM((exp_local, rank, hidden), BF16),
            pltpu.SemaphoreType.DMA((4, 2)),
        ],
        compiler_params=pltpu.CompilerParams(vmem_limit_bytes=VL_L),
        cost_estimate=pl.CostEstimate(
            flops=2 * exp_local * rows * hidden * rank,
            bytes_accessed=2 * exp_local * hidden * (rows + rank),
            transcendentals=0,
        ),
    )(hidden_grad, proj_out.transpose(0, 2, 1))

    me = jnp.stack([lax.axis_index("expert"), lax.axis_index("dp")]).astype(jnp.int32)
    smem = pl.BlockSpec(memory_space=pltpu.SMEM)
    block = jax.ShapeDtypeStruct((DOC_GRP, chunks, exp_local, LANES), BF16)
    feats = pl.pallas_call(
        functools.partial(feature_kernel, groups, dp, rank, top),
        out_shape=(block,) * dp,
        in_specs=[smem] + [vmem] * (groups + 1),
        out_specs=(vmem,) * dp,
        scratch_shapes=[
            pltpu.VMEM((exp_local, rows, 2 * rank), BF16),
            pltpu.VMEM((DOC_GRP * rank // 2 * exp_local, 2 * rank), F32),
        ],
        compiler_params=pltpu.CompilerParams(vmem_limit_bytes=VL_F),
        cost_estimate=pl.CostEstimate(
            flops=8 * exp_local * rows * rank * tok, bytes_accessed=1 << 20, transcendentals=0
        ),
    )(me, *pays, low)
    arrived = [feats[0]]
    for k in range(1, dp):
        arrived.append(lax.ppermute(feats[k], "dp", [(a, a ^ k) for a in range(dp)]))

    scale = 1.0 / float(experts * entries) ** 0.5
    part = pl.pallas_call(
        functools.partial(score_kernel, dp, scale),
        out_shape=jax.ShapeDtypeStruct((groups * dp, DOC_GRP, dp * vals), F32),
        in_specs=[smem] + [vmem] * (dp + 1),
        out_specs=vmem,
        compiler_params=pltpu.CompilerParams(vmem_limit_bytes=40 << 20),
    )(me, *arrived, val_all)
    parts = lax.all_to_all(part, ("expert", "dp"), split_axis=0, concat_axis=0, tiled=True)
    return jnp.sum(parts, axis=0)


def solution(mesh):
    in_specs = (
        P(("expert", "dp"), None),
        P(("expert", "dp"), None),
        P(("expert", "dp"), None),
        P(("expert", "dp")),
        P("expert", "dp", None),
        P(),
        P("expert", None, None),
        P("dp", "expert", None),
    )
    out_specs = P("dp", None)
    return jax.shard_map(layer, mesh=mesh, in_specs=in_specs, out_specs=out_specs, check_vma=False)
```

```python
import functools

import jax
import jax.numpy as jnp
from jax import lax
from jax.experimental import pallas as pl
from jax.experimental.pallas import tpu as pltpu
from jax.sharding import Mesh
from jax.sharding import PartitionSpec as P


DOC_GRP = 2
SPLIT = 4
LANES = 128
VL_A = 63 << 20
VL_L = 53 << 20
VL_F = 16 << 20
F32 = jnp.float32
BF16 = jnp.bfloat16
NT = (((1,), (1,)), ((), ()))
TN = (((0,), (0,)), ((), ()))


def split_kernel(val_hbm, out_hbm, piece_ref, in_sems, out_sems):
    parts, _, _, piece = piece_ref.shape
    ins = []
    for j in range(parts):
        cols = pl.ds(j * piece, piece)
        ins.append(pltpu.make_async_copy(val_hbm.at[:, :, cols], piece_ref.at[j], in_sems.at[j]))
        ins[j].start()
    outs = []
    for j in range(parts):
        ins[j].wait()
        for t in range(j, out_hbm.shape[0], parts):
            outs.append(
                pltpu.make_async_copy(piece_ref.at[j], out_hbm.at[t], out_sems.at[t])
            )
            outs[-1].start()
    for copy in outs:
        copy.wait()


def act_kernel(tok_hbm, proj_hbm, routes_hbm, gates_hbm, docs_hbm, out_ref, *scratch):
    tok_ref, proj_ref, routes_ref, gates_ref, docs_ref, acc_ref, sems, small_sems = scratch
    rank = proj_ref.shape[0]
    top = routes_ref.shape[0]
    half = rank // 2
    steps = sems.shape[0]
    width = tok_ref.shape[1] // steps
    copies = []
    for s in range(steps):
        cols = pl.ds(s * width, width)
        copies.append(
            (
                pltpu.make_async_copy(proj_hbm.at[:, cols], proj_ref.at[:, cols], sems.at[s, 0]),
                pltpu.make_async_copy(tok_hbm.at[:, cols], tok_ref.at[:, cols], sems.at[s, 1]),
            )
        )
    smalls = [
        pltpu.make_async_copy(routes_hbm, routes_ref, small_sems.at[0]),
        pltpu.make_async_copy(gates_hbm, gates_ref, small_sems.at[1]),
        pltpu.make_async_copy(docs_hbm, docs_ref, small_sems.at[2]),
    ]
    for copy in copies[0]:
        copy.start()
    for copy in smalls:
        copy.start()
    for pair in copies[1:]:
        for copy in pair:
            copy.start()
    for copy in smalls:
        copy.wait()
    out_ref[rank : rank + top, :] = routes_ref[...].astype(F32)
    out_ref[rank + top : rank + 2 * top, :] = gates_ref[...]
    out_ref[rank + 2 * top :, :] = jnp.broadcast_to(
        docs_ref[...].astype(F32), (out_ref.shape[0] - rank - 2 * top, out_ref.shape[1])
    )
    total = jnp.zeros(acc_ref.shape, F32)
    for s in range(steps):
        for copy in copies[s]:
            copy.wait()
        cols = slice(s * width, (s + 1) * width)
        total += lax.dot_general(
            proj_ref[:, cols], tok_ref[:, cols], NT, preferred_element_type=F32
        )
    acc_ref[...] = total
    out_ref[0:half, :] = acc_ref[pl.ds(0, half, stride=2), :]
    out_ref[half:rank, :] = acc_ref[pl.ds(1, half, stride=2), :]


def lowered_kernel(grad_hbm, proj_hbm, out_ref, grad_ref, proj_ref, sems):
    count = sems.shape[0]
    batch = grad_ref.shape[0] // count
    copies = []
    for n in range(count):
        part = pl.ds(n * batch, batch)
        copies.append(
            (
                pltpu.make_async_copy(proj_hbm.at[part], proj_ref.at[part], sems.at[n, 0]),
                pltpu.make_async_copy(grad_hbm.at[part], grad_ref.at[part], sems.at[n, 1]),
            )
        )
    for pair in copies:
        for copy in pair:
            copy.start()
    for n in range(count):
        for copy in copies[n]:
            copy.wait()
        for e in range(n * batch, (n + 1) * batch):
            low = lax.dot_general(grad_ref[e], proj_ref[e], NT, preferred_element_type=F32)
            out_ref[e] = jnp.concatenate([low, low], axis=1).astype(BF16)


def feature_kernel(groups, parts, rank, top, me_ref, mine_ref, *refs):
    pays = refs[:groups]
    low_ref = refs[groups]
    outs = refs[groups + 1 : groups + 1 + parts]
    a_ref, f_ref = refs[groups + 1 + parts :]
    exp_local, rows, _ = low_ref.shape
    cap = rows // groups
    tok = pays[0].shape[1]
    half = rank // 2
    me = me_ref[0]
    base = (me * exp_local).astype(F32)
    experts = lax.broadcasted_iota(jnp.int32, (exp_local, tok), 0).astype(F32) + base
    before = (
        lax.broadcasted_iota(jnp.int32, (tok, tok), 0)
        < lax.broadcasted_iota(jnp.int32, (tok, tok), 1)
    ).astype(BF16)
    slots = lax.broadcasted_iota(jnp.int32, (cap, tok), 0).astype(F32)
    for k in range(groups):
        pay = pays[k]
        hit = jnp.zeros((exp_local, tok), F32)
        gate = jnp.zeros((exp_local, tok), F32)
        for t in range(top):
            same = pay[rank + t : rank + t + 1, :] == experts
            hit = jnp.where(same, 1.0, hit)
            gate = jnp.where(same, pay[rank + top + t : rank + top + t + 1, :], gate)
        slot = jnp.dot(hit.astype(BF16), before, preferred_element_type=F32)
        slot = jnp.where(hit > 0.0, slot, -1.0)
        doc = pay[rank + 2 * top : rank + 2 * top + 1, :]
        masked = []
        for par in range(2):
            act = pay[par * half : (par + 1) * half, :]
            for d in range(DOC_GRP):
                masked.append(jnp.where(doc == float(d), act, 0.0))
        act = jnp.concatenate(masked, axis=0)
        high = act.astype(BF16)
        low = (act - high.astype(F32)).astype(BF16)
        right = jnp.concatenate([high, low], axis=1)
        picks, scales = [], []
        for e in range(exp_local):
            pick = slot[e : e + 1, :] == slots
            picks.append(jnp.where(pick, 1.0, 0.0).astype(BF16))
            scales.append(
                jnp.sum(jnp.where(pick, gate[e : e + 1, :], 0.0), axis=1, keepdims=True)
            )
        left = jnp.concatenate(picks, axis=0)
        scale = jnp.concatenate(scales, axis=0)
        left = jnp.concatenate([left, left], axis=1)
        sent = lax.dot_general(left, right, NT, preferred_element_type=F32) * scale
        sent = sent.astype(BF16)
        source = pl.multiple_of(lax.bitwise_xor(me, k) * cap, cap)
        for e in range(exp_local):
            a_ref[e, pl.ds(source, cap), :] = sent[e * cap : (e + 1) * cap, :]
    wide = DOC_GRP * half
    lane = lax.broadcasted_iota(jnp.int32, (wide, 2 * rank), 1)
    for e in range(exp_local):
        feat = lax.dot_general(a_ref[e], low_ref[e], TN, preferred_element_type=F32)
        f_ref[pl.ds(e, wide, stride=exp_local), :] = jnp.where(
            lane < rank, feat[:wide], feat[wide:]
        )
    _, chunks, _, _ = outs[0].shape
    size = chunks * exp_local
    for k in range(parts):
        part = lax.bitwise_xor(mine_ref[0], k)
        for d in range(DOC_GRP):
            start = pl.multiple_of((d * half + part * chunks) * exp_local, size)
            outs[k][d] = (
                f_ref[pl.ds(start, size), :].astype(BF16).reshape(chunks, exp_local, 2 * rank)
            )


def score_kernel(parts, scale, mine_ref, *refs):
    feats, val_ref, out_ref = refs[:parts], refs[parts], refs[parts + 1]
    docs, chunks, exp_local, lanes = feats[0].shape
    vals = val_ref.shape[0] * val_ref.shape[1]
    left_rows, right_rows = parts * docs * exp_local, vals * exp_local
    total = jnp.zeros((left_rows, right_rows), F32)
    for c in range(chunks):
        left = jnp.concatenate(
            [feat[:, c].reshape(docs * exp_local, lanes) for feat in feats], axis=0
        )
        right = val_ref[:, :, :, c * lanes : (c + 1) * lanes].reshape(right_rows, lanes)
        total += lax.dot_general(left, right, NT, preferred_element_type=F32)
    row = lax.broadcasted_iota(jnp.int32, total.shape, 0) % exp_local
    col = lax.broadcasted_iota(jnp.int32, total.shape, 1) % exp_local
    total = jnp.where(row == col, total, 0.0)
    total = jnp.sum(total.reshape(parts * docs, exp_local, right_rows), axis=1)
    pick = (
        lax.broadcasted_iota(jnp.int32, (right_rows, vals), 0) // exp_local
        == lax.broadcasted_iota(jnp.int32, (right_rows, vals), 1)
    ).astype(F32)
    scores = jnp.dot(
        total, pick, preferred_element_type=F32, precision=lax.Precision.HIGHEST
    ) * scale
    for k in range(parts):
        group = lax.bitwise_xor(mine_ref[0], k)
        for i in range(out_ref.shape[0] // parts):
            out_ref[i * parts + group] = scores[k * docs : (k + 1) * docs, :]


def layer(tokens, gates, routes, doc_ids, hidden_grad, proj_in, proj_out, val_features):
    tok, width = tokens.shape
    top = routes.shape[1]
    rank = proj_in.shape[1]
    groups = lax.axis_size("expert")
    lo = lax.axis_size("lo")
    dp = lax.axis_size("hi") * lo
    exp_local, rows, hidden = hidden_grad.shape
    vals = val_features.shape[0]
    entries = rank * rank
    experts = exp_local * groups
    chunks = entries // LANES // lo

    vmem = pl.BlockSpec(memory_space=pltpu.VMEM)
    hbm = pl.BlockSpec(memory_space=pltpu.HBM)
    val_split = pl.pallas_call(
        split_kernel,
        out_shape=jax.ShapeDtypeStruct((dp, vals, exp_local, entries // lo), BF16),
        in_specs=[hbm],
        out_specs=hbm,
        scratch_shapes=[
            pltpu.VMEM((lo, vals, exp_local, entries // lo), BF16),
            pltpu.SemaphoreType.DMA((lo,)),
            pltpu.SemaphoreType.DMA((dp,)),
        ],
        compiler_params=pltpu.CompilerParams(vmem_limit_bytes=VL_A),
    )(val_features)
    val_all = lax.all_to_all(
        val_split, ("hi", "lo"), split_axis=0, concat_axis=0, tiled=True
    )

    pay_rows = rank + 2 * top + 8
    steps = 2
    pay = pl.pallas_call(
        act_kernel,
        out_shape=jax.ShapeDtypeStruct((pay_rows, tok), F32),
        in_specs=[hbm] * 5,
        out_specs=vmem,
        scratch_shapes=[
            pltpu.VMEM((tok, width), BF16),
            pltpu.VMEM((rank, width), BF16),
            pltpu.VMEM((top, tok), jnp.int32),
            pltpu.VMEM((top, tok), F32),
            pltpu.VMEM((1, tok), jnp.int32),
            pltpu.VMEM((rank, tok), F32),
            pltpu.SemaphoreType.DMA((steps, 2)),
            pltpu.SemaphoreType.DMA((3,)),
        ],
        compiler_params=pltpu.CompilerParams(vmem_limit_bytes=VL_A),
        cost_estimate=pl.CostEstimate(
            flops=2 * tok * width * rank,
            bytes_accessed=2 * width * (tok + rank),
            transcendentals=0,
        ),
    )(tokens, proj_in.T, routes.T, gates.T, doc_ids.reshape(1, tok))

    pays = [pay]
    for k in range(1, groups):
        pays.append(lax.ppermute(pay, "expert", [(a, a ^ k) for a in range(groups)]))

    low = pl.pallas_call(
        lowered_kernel,
        out_shape=jax.ShapeDtypeStruct((exp_local, rows, 2 * rank), BF16),
        in_specs=[hbm, hbm],
        out_specs=vmem,
        scratch_shapes=[
            pltpu.VMEM((exp_local, rows, hidden), BF16),
            pltpu.VMEM((exp_local, rank, hidden), BF16),
            pltpu.SemaphoreType.DMA((4, 2)),
        ],
        compiler_params=pltpu.CompilerParams(vmem_limit_bytes=VL_L),
        cost_estimate=pl.CostEstimate(
            flops=2 * exp_local * rows * hidden * rank,
            bytes_accessed=2 * exp_local * hidden * (rows + rank),
            transcendentals=0,
        ),
    )(hidden_grad, proj_out.transpose(0, 2, 1))

    me = lax.axis_index("expert").astype(jnp.int32).reshape(1)
    mine = lax.axis_index("lo").astype(jnp.int32).reshape(1)
    smem = pl.BlockSpec(memory_space=pltpu.SMEM)
    block = jax.ShapeDtypeStruct((DOC_GRP, chunks, exp_local, LANES), BF16)
    feats = pl.pallas_call(
        functools.partial(feature_kernel, groups, lo, rank, top),
        out_shape=(block,) * lo,
        in_specs=[smem, smem] + [vmem] * (groups + 1),
        out_specs=(vmem,) * lo,
        scratch_shapes=[
            pltpu.VMEM((exp_local, rows, 2 * rank), BF16),
            pltpu.VMEM((DOC_GRP * rank // 2 * exp_local, 2 * rank), F32),
        ],
        compiler_params=pltpu.CompilerParams(vmem_limit_bytes=VL_F),
        cost_estimate=pl.CostEstimate(
            flops=8 * exp_local * rows * rank * tok, bytes_accessed=1 << 20, transcendentals=0
        ),
    )(me, mine, *pays, low)
    arrived = [feats[0]]
    for k in range(1, lo):
        arrived.append(lax.ppermute(feats[k], "lo", [(a, a ^ k) for a in range(lo)]))

    scale = 1.0 / float(experts * entries) ** 0.5
    part = pl.pallas_call(
        functools.partial(score_kernel, lo, scale),
        out_shape=jax.ShapeDtypeStruct((groups * lo, DOC_GRP, dp * vals), F32),
        in_specs=[smem] + [vmem] * (lo + 1),
        out_specs=vmem,
        compiler_params=pltpu.CompilerParams(vmem_limit_bytes=40 << 20),
    )(mine, *arrived, val_all)
    parts = lax.all_to_all(part, ("expert", "lo"), split_axis=0, concat_axis=0, tiled=True)
    return jnp.sum(parts, axis=0)


def solution(mesh):
    groups, dp = mesh.shape["expert"], mesh.shape["dp"]
    lo = min(SPLIT, dp)
    grid = Mesh(mesh.devices.reshape(groups, dp // lo, lo), ("expert", "hi", "lo"))
    everyone = ("expert", "hi", "lo")
    in_specs = (
        P(everyone, None),
        P(everyone, None),
        P(everyone, None),
        P(everyone),
        P("expert", ("hi", "lo"), None),
        P(),
        P("expert", None, None),
        P(("hi", "lo"), "expert", None),
    )
    out_specs = P(("hi", "lo"), None)
    return jax.shard_map(layer, mesh=grid, in_specs=in_specs, out_specs=out_specs, check_vma=False)
```

```python
import functools

import jax
import jax.numpy as jnp
from jax import lax
from jax.experimental import pallas as pl
from jax.experimental.pallas import tpu as pltpu
from jax.sharding import Mesh
from jax.sharding import PartitionSpec as P


DOC_GRP = 2
SPLIT = 4
LANES = 128
VL_A = 63 << 20
VL_L = 53 << 20
VL_F = 16 << 20
F32 = jnp.float32
BF16 = jnp.bfloat16
NT = (((1,), (1,)), ((), ()))
TN = (((0,), (0,)), ((), ()))


def split_kernel(mine_ref, val_hbm, *refs):
    outs, (piece_ref, sems) = refs[:-2], refs[-2:]
    parts, _, _, piece = piece_ref.shape
    ins, puts = [], []
    for k in range(parts):
        part = lax.bitwise_xor(mine_ref[0], k)
        cols = pl.ds(pl.multiple_of(part * piece, piece), piece)
        ins.append(pltpu.make_async_copy(val_hbm.at[:, :, cols], piece_ref.at[k], sems.at[k, 0]))
        puts.append(pltpu.make_async_copy(piece_ref.at[k], outs[k], sems.at[k, 1]))
    for copy in ins:
        copy.start()
    for k in range(parts):
        ins[k].wait()
        puts[k].start()
    for copy in puts:
        copy.wait()


def act_kernel(tok_hbm, proj_hbm, routes_hbm, gates_hbm, docs_hbm, out_ref, *scratch):
    tok_ref, proj_ref, routes_ref, gates_ref, docs_ref, acc_ref, sems, small_sems = scratch
    rank = proj_ref.shape[0]
    top = routes_ref.shape[0]
    half = rank // 2
    steps = sems.shape[0]
    width = tok_ref.shape[1] // steps
    copies = []
    for s in range(steps):
        cols = pl.ds(s * width, width)
        copies.append(
            (
                pltpu.make_async_copy(proj_hbm.at[:, cols], proj_ref.at[:, cols], sems.at[s, 0]),
                pltpu.make_async_copy(tok_hbm.at[:, cols], tok_ref.at[:, cols], sems.at[s, 1]),
            )
        )
    smalls = [
        pltpu.make_async_copy(routes_hbm, routes_ref, small_sems.at[0]),
        pltpu.make_async_copy(gates_hbm, gates_ref, small_sems.at[1]),
        pltpu.make_async_copy(docs_hbm, docs_ref, small_sems.at[2]),
    ]
    for copy in copies[0]:
        copy.start()
    for copy in smalls:
        copy.start()
    for pair in copies[1:]:
        for copy in pair:
            copy.start()
    for copy in smalls:
        copy.wait()
    out_ref[rank : rank + top, :] = routes_ref[...].astype(F32)
    out_ref[rank + top : rank + 2 * top, :] = gates_ref[...]
    out_ref[rank + 2 * top :, :] = jnp.broadcast_to(
        docs_ref[...].astype(F32), (out_ref.shape[0] - rank - 2 * top, out_ref.shape[1])
    )
    total = jnp.zeros(acc_ref.shape, F32)
    for s in range(steps):
        for copy in copies[s]:
            copy.wait()
        cols = slice(s * width, (s + 1) * width)
        total += lax.dot_general(
            proj_ref[:, cols], tok_ref[:, cols], NT, preferred_element_type=F32
        )
    acc_ref[...] = total
    out_ref[0:half, :] = acc_ref[pl.ds(0, half, stride=2), :]
    out_ref[half:rank, :] = acc_ref[pl.ds(1, half, stride=2), :]


def lowered_kernel(grad_hbm, proj_hbm, out_ref, grad_ref, proj_ref, sems):
    count = sems.shape[0]
    batch = grad_ref.shape[0] // count
    copies = []
    for n in range(count):
        part = pl.ds(n * batch, batch)
        copies.append(
            (
                pltpu.make_async_copy(proj_hbm.at[part], proj_ref.at[part], sems.at[n, 0]),
                pltpu.make_async_copy(grad_hbm.at[part], grad_ref.at[part], sems.at[n, 1]),
            )
        )
    for pair in copies:
        for copy in pair:
            copy.start()
    for n in range(count):
        for copy in copies[n]:
            copy.wait()
        for e in range(n * batch, (n + 1) * batch):
            low = lax.dot_general(grad_ref[e], proj_ref[e], NT, preferred_element_type=F32)
            out_ref[e] = jnp.concatenate([low, low], axis=1).astype(BF16)


def feature_kernel(groups, parts, rank, top, me_ref, mine_ref, *refs):
    pays = refs[:groups]
    low_ref = refs[groups]
    outs = refs[groups + 1 : groups + 1 + parts]
    a_ref, f_ref = refs[groups + 1 + parts :]
    exp_local, rows, _ = low_ref.shape
    cap = rows // groups
    tok = pays[0].shape[1]
    half = rank // 2
    me = me_ref[0]
    base = (me * exp_local).astype(F32)
    experts = lax.broadcasted_iota(jnp.int32, (exp_local, tok), 0).astype(F32) + base
    before = (
        lax.broadcasted_iota(jnp.int32, (tok, tok), 0)
        < lax.broadcasted_iota(jnp.int32, (tok, tok), 1)
    ).astype(BF16)
    slots = lax.broadcasted_iota(jnp.int32, (cap, tok), 0).astype(F32)
    for k in range(groups):
        pay = pays[k]
        hit = jnp.zeros((exp_local, tok), F32)
        gate = jnp.zeros((exp_local, tok), F32)
        for t in range(top):
            same = pay[rank + t : rank + t + 1, :] == experts
            hit = jnp.where(same, 1.0, hit)
            gate = jnp.where(same, pay[rank + top + t : rank + top + t + 1, :], gate)
        slot = jnp.dot(hit.astype(BF16), before, preferred_element_type=F32)
        slot = jnp.where(hit > 0.0, slot, -1.0)
        doc = pay[rank + 2 * top : rank + 2 * top + 1, :]
        masked = []
        for par in range(2):
            act = pay[par * half : (par + 1) * half, :]
            for d in range(DOC_GRP):
                masked.append(jnp.where(doc == float(d), act, 0.0))
        act = jnp.concatenate(masked, axis=0)
        high = act.astype(BF16)
        low = (act - high.astype(F32)).astype(BF16)
        right = jnp.concatenate([high, low], axis=1)
        picks, scales = [], []
        for e in range(exp_local):
            pick = slot[e : e + 1, :] == slots
            picks.append(jnp.where(pick, 1.0, 0.0).astype(BF16))
            scales.append(
                jnp.sum(jnp.where(pick, gate[e : e + 1, :], 0.0), axis=1, keepdims=True)
            )
        left = jnp.concatenate(picks, axis=0)
        scale = jnp.concatenate(scales, axis=0)
        left = jnp.concatenate([left, left], axis=1)
        sent = lax.dot_general(left, right, NT, preferred_element_type=F32) * scale
        sent = sent.astype(BF16)
        source = pl.multiple_of(lax.bitwise_xor(me, k) * cap, cap)
        for e in range(exp_local):
            a_ref[e, pl.ds(source, cap), :] = sent[e * cap : (e + 1) * cap, :]
    wide = DOC_GRP * half
    lane = lax.broadcasted_iota(jnp.int32, (wide, 2 * rank), 1)
    for e in range(exp_local):
        feat = lax.dot_general(a_ref[e], low_ref[e], TN, preferred_element_type=F32)
        f_ref[pl.ds(e, wide, stride=exp_local), :] = jnp.where(
            lane < rank, feat[:wide], feat[wide:]
        )
    _, chunks, _, _ = outs[0].shape
    size = chunks * exp_local
    for k in range(parts):
        part = lax.bitwise_xor(mine_ref[0], k)
        for d in range(DOC_GRP):
            start = pl.multiple_of((d * half + part * chunks) * exp_local, size)
            outs[k][d] = (
                f_ref[pl.ds(start, size), :].astype(BF16).reshape(chunks, exp_local, 2 * rank)
            )


def score_kernel(parts, scale, mine_ref, *refs):
    feats, pieces, out_ref = refs[:parts], refs[parts:-1], refs[-1]
    docs, chunks, exp_local, lanes = feats[0].shape
    each = pieces[0].shape[0]
    vals = len(pieces) * each
    left_rows, right_rows = parts * docs * exp_local, vals * exp_local
    total = jnp.zeros((left_rows, right_rows), F32)
    for c in range(chunks):
        left = jnp.concatenate(
            [feat[:, c].reshape(docs * exp_local, lanes) for feat in feats], axis=0
        )
        right = jnp.concatenate(
            [
                val[:, :, c * lanes : (c + 1) * lanes].reshape(each * exp_local, lanes)
                for val in pieces
            ],
            axis=0,
        )
        total += lax.dot_general(left, right, NT, preferred_element_type=F32)
    row = lax.broadcasted_iota(jnp.int32, total.shape, 0) % exp_local
    col = lax.broadcasted_iota(jnp.int32, total.shape, 1) % exp_local
    total = jnp.where(row == col, total, 0.0)
    total = jnp.sum(total.reshape(parts * docs, exp_local, right_rows), axis=1)
    owner = lax.broadcasted_iota(jnp.int32, (right_rows, vals), 0) // exp_local
    owner = lax.bitwise_xor(owner, mine_ref[0] * each)
    pick = (owner == lax.broadcasted_iota(jnp.int32, (right_rows, vals), 1)).astype(F32)
    scores = jnp.dot(
        total, pick, preferred_element_type=F32, precision=lax.Precision.HIGHEST
    ) * scale
    for k in range(parts):
        group = lax.bitwise_xor(mine_ref[0] % parts, k)
        for i in range(out_ref.shape[0] // parts):
            out_ref[i * parts + group] = scores[k * docs : (k + 1) * docs, :]


def layer(tokens, gates, routes, doc_ids, hidden_grad, proj_in, proj_out, val_features):
    tok, width = tokens.shape
    top = routes.shape[1]
    rank = proj_in.shape[1]
    groups = lax.axis_size("expert")
    lo = lax.axis_size("lo")
    dp = lax.axis_size("hi") * lo
    exp_local, rows, hidden = hidden_grad.shape
    vals = val_features.shape[0]
    entries = rank * rank
    experts = exp_local * groups
    chunks = entries // LANES // lo

    vmem = pl.BlockSpec(memory_space=pltpu.VMEM)
    hbm = pl.BlockSpec(memory_space=pltpu.HBM)
    smem = pl.BlockSpec(memory_space=pltpu.SMEM)
    mine = lax.axis_index("lo").astype(jnp.int32).reshape(1)
    pieces = pl.pallas_call(
        split_kernel,
        out_shape=(jax.ShapeDtypeStruct((vals, exp_local, entries // lo), BF16),) * lo,
        in_specs=[smem, hbm],
        out_specs=(hbm,) * lo,
        scratch_shapes=[
            pltpu.VMEM((lo, vals, exp_local, entries // lo), BF16),
            pltpu.SemaphoreType.DMA((lo, 2)),
        ],
        compiler_params=pltpu.CompilerParams(vmem_limit_bytes=VL_A),
    )(mine, val_features)
    val_all = [pieces[0]] * dp
    for k in range(dp - 1, 0, -1):
        val_all[k] = lax.ppermute(
            pieces[k % lo], ("hi", "lo"), [(a, a ^ k) for a in range(dp)]
        )

    pay_rows = rank + 2 * top + 8
    steps = 2
    pay = pl.pallas_call(
        act_kernel,
        out_shape=jax.ShapeDtypeStruct((pay_rows, tok), F32),
        in_specs=[hbm] * 5,
        out_specs=vmem,
        scratch_shapes=[
            pltpu.VMEM((tok, width), BF16),
            pltpu.VMEM((rank, width), BF16),
            pltpu.VMEM((top, tok), jnp.int32),
            pltpu.VMEM((top, tok), F32),
            pltpu.VMEM((1, tok), jnp.int32),
            pltpu.VMEM((rank, tok), F32),
            pltpu.SemaphoreType.DMA((steps, 2)),
            pltpu.SemaphoreType.DMA((3,)),
        ],
        compiler_params=pltpu.CompilerParams(vmem_limit_bytes=VL_A),
        cost_estimate=pl.CostEstimate(
            flops=2 * tok * width * rank,
            bytes_accessed=2 * width * (tok + rank),
            transcendentals=0,
        ),
    )(tokens, proj_in.T, routes.T, gates.T, doc_ids.reshape(1, tok))

    pays = [pay]
    for k in range(1, groups):
        pays.append(lax.ppermute(pay, "expert", [(a, a ^ k) for a in range(groups)]))

    low = pl.pallas_call(
        lowered_kernel,
        out_shape=jax.ShapeDtypeStruct((exp_local, rows, 2 * rank), BF16),
        in_specs=[hbm, hbm],
        out_specs=vmem,
        scratch_shapes=[
            pltpu.VMEM((exp_local, rows, hidden), BF16),
            pltpu.VMEM((exp_local, rank, hidden), BF16),
            pltpu.SemaphoreType.DMA((4, 2)),
        ],
        compiler_params=pltpu.CompilerParams(vmem_limit_bytes=VL_L),
        cost_estimate=pl.CostEstimate(
            flops=2 * exp_local * rows * hidden * rank,
            bytes_accessed=2 * exp_local * hidden * (rows + rank),
            transcendentals=0,
        ),
    )(hidden_grad, proj_out.transpose(0, 2, 1))

    me = lax.axis_index("expert").astype(jnp.int32).reshape(1)
    block = jax.ShapeDtypeStruct((DOC_GRP, chunks, exp_local, LANES), BF16)
    feats = pl.pallas_call(
        functools.partial(feature_kernel, groups, lo, rank, top),
        out_shape=(block,) * lo,
        in_specs=[smem, smem] + [vmem] * (groups + 1),
        out_specs=(vmem,) * lo,
        scratch_shapes=[
            pltpu.VMEM((exp_local, rows, 2 * rank), BF16),
            pltpu.VMEM((DOC_GRP * rank // 2 * exp_local, 2 * rank), F32),
        ],
        compiler_params=pltpu.CompilerParams(vmem_limit_bytes=VL_F),
        cost_estimate=pl.CostEstimate(
            flops=8 * exp_local * rows * rank * tok, bytes_accessed=1 << 20, transcendentals=0
        ),
    )(me, mine, *pays, low)
    arrived = [feats[0]]
    for k in range(1, lo):
        arrived.append(lax.ppermute(feats[k], "lo", [(a, a ^ k) for a in range(lo)]))

    scale = 1.0 / float(experts * entries) ** 0.5
    part = pl.pallas_call(
        functools.partial(score_kernel, lo, scale),
        out_shape=jax.ShapeDtypeStruct((groups * lo, DOC_GRP, dp * vals), F32),
        in_specs=[smem] + [vmem] * (lo + dp),
        out_specs=vmem,
        compiler_params=pltpu.CompilerParams(vmem_limit_bytes=40 << 20),
    )(lax.axis_index(("hi", "lo")).astype(jnp.int32).reshape(1), *arrived, *val_all)
    parts = lax.all_to_all(part, ("expert", "lo"), split_axis=0, concat_axis=0, tiled=True)
    return jnp.sum(parts, axis=0)


def solution(mesh):
    groups, dp = mesh.shape["expert"], mesh.shape["dp"]
    lo = min(SPLIT, dp)
    grid = Mesh(mesh.devices.reshape(groups, dp // lo, lo), ("expert", "hi", "lo"))
    everyone = ("expert", "hi", "lo")
    in_specs = (
        P(everyone, None),
        P(everyone, None),
        P(everyone, None),
        P(everyone),
        P("expert", ("hi", "lo"), None),
        P(),
        P("expert", None, None),
        P(("hi", "lo"), "expert", None),
    )
    out_specs = P(("hi", "lo"), None)
    return jax.shard_map(layer, mesh=grid, in_specs=in_specs, out_specs=out_specs, check_vma=False)
```

```python
import functools

import jax
import jax.numpy as jnp
from jax import lax
from jax.experimental import pallas as pl
from jax.experimental.pallas import tpu as pltpu
from jax.sharding import Mesh
from jax.sharding import PartitionSpec as P


DOC_GRP = 2
SPLIT = 4
LANES = 128
VL_A = 63 << 20
VL_L = 53 << 20
VL_F = 16 << 20
F32 = jnp.float32
BF16 = jnp.bfloat16
NT = (((1,), (1,)), ((), ()))
TN = (((0,), (0,)), ((), ()))


def start_order(dp, lo):
    return sorted(range(dp - 1, 0, -1), key=lambda k: (k < lo, k % 2 if k >= lo else 0))


def act_kernel(tok_hbm, proj_hbm, routes_hbm, gates_hbm, docs_hbm, out_ref, *scratch):
    tok_ref, proj_ref, routes_ref, gates_ref, docs_ref, acc_ref, sems, small_sems = scratch
    rank = proj_ref.shape[0]
    top = routes_ref.shape[0]
    half = rank // 2
    steps = sems.shape[0]
    width = tok_ref.shape[1] // steps
    copies = []
    for s in range(steps):
        cols = pl.ds(s * width, width)
        copies.append(
            (
                pltpu.make_async_copy(proj_hbm.at[:, cols], proj_ref.at[:, cols], sems.at[s, 0]),
                pltpu.make_async_copy(tok_hbm.at[:, cols], tok_ref.at[:, cols], sems.at[s, 1]),
            )
        )
    smalls = [
        pltpu.make_async_copy(routes_hbm, routes_ref, small_sems.at[0]),
        pltpu.make_async_copy(gates_hbm, gates_ref, small_sems.at[1]),
        pltpu.make_async_copy(docs_hbm, docs_ref, small_sems.at[2]),
    ]
    for copy in copies[0]:
        copy.start()
    for copy in smalls:
        copy.start()
    for pair in copies[1:]:
        for copy in pair:
            copy.start()
    for copy in smalls:
        copy.wait()
    out_ref[rank : rank + top, :] = routes_ref[...].astype(F32)
    out_ref[rank + top : rank + 2 * top, :] = gates_ref[...]
    out_ref[rank + 2 * top :, :] = jnp.broadcast_to(
        docs_ref[...].astype(F32), (out_ref.shape[0] - rank - 2 * top, out_ref.shape[1])
    )
    total = jnp.zeros(acc_ref.shape, F32)
    for s in range(steps):
        for copy in copies[s]:
            copy.wait()
        cols = slice(s * width, (s + 1) * width)
        total += lax.dot_general(
            proj_ref[:, cols], tok_ref[:, cols], NT, preferred_element_type=F32
        )
    acc_ref[...] = total
    out_ref[0:half, :] = acc_ref[pl.ds(0, half, stride=2), :]
    out_ref[half:rank, :] = acc_ref[pl.ds(1, half, stride=2), :]


def lowered_kernel(grad_hbm, proj_hbm, out_ref, grad_ref, proj_ref, sems):
    count = sems.shape[0]
    batch = grad_ref.shape[0] // count
    copies = []
    for n in range(count):
        part = pl.ds(n * batch, batch)
        copies.append(
            (
                pltpu.make_async_copy(proj_hbm.at[part], proj_ref.at[part], sems.at[n, 0]),
                pltpu.make_async_copy(grad_hbm.at[part], grad_ref.at[part], sems.at[n, 1]),
            )
        )
    for pair in copies:
        for copy in pair:
            copy.start()
    for n in range(count):
        for copy in copies[n]:
            copy.wait()
        for e in range(n * batch, (n + 1) * batch):
            low = lax.dot_general(grad_ref[e], proj_ref[e], NT, preferred_element_type=F32)
            out_ref[e] = jnp.concatenate([low, low], axis=1).astype(BF16)


def feature_kernel(groups, parts, rank, top, me_ref, mine_ref, *refs):
    pays = refs[:groups]
    low_ref = refs[groups]
    outs = refs[groups + 1 : groups + 1 + parts]
    a_ref, f_ref = refs[groups + 1 + parts :]
    exp_local, rows, _ = low_ref.shape
    cap = rows // groups
    tok = pays[0].shape[1]
    half = rank // 2
    me = me_ref[0]
    base = (me * exp_local).astype(F32)
    experts = lax.broadcasted_iota(jnp.int32, (exp_local, tok), 0).astype(F32) + base
    before = (
        lax.broadcasted_iota(jnp.int32, (tok, tok), 0)
        < lax.broadcasted_iota(jnp.int32, (tok, tok), 1)
    ).astype(BF16)
    slots = lax.broadcasted_iota(jnp.int32, (cap, tok), 0).astype(F32)
    for k in range(groups):
        pay = pays[k]
        hit = jnp.zeros((exp_local, tok), F32)
        gate = jnp.zeros((exp_local, tok), F32)
        for t in range(top):
            same = pay[rank + t : rank + t + 1, :] == experts
            hit = jnp.where(same, 1.0, hit)
            gate = jnp.where(same, pay[rank + top + t : rank + top + t + 1, :], gate)
        slot = jnp.dot(hit.astype(BF16), before, preferred_element_type=F32)
        slot = jnp.where(hit > 0.0, slot, -1.0)
        doc = pay[rank + 2 * top : rank + 2 * top + 1, :]
        masked = []
        for par in range(2):
            act = pay[par * half : (par + 1) * half, :]
            for d in range(DOC_GRP):
                masked.append(jnp.where(doc == float(d), act, 0.0))
        act = jnp.concatenate(masked, axis=0)
        high = act.astype(BF16)
        low = (act - high.astype(F32)).astype(BF16)
        right = jnp.concatenate([high, low], axis=1)
        picks, scales = [], []
        for e in range(exp_local):
            pick = slot[e : e + 1, :] == slots
            picks.append(jnp.where(pick, 1.0, 0.0).astype(BF16))
            scales.append(
                jnp.sum(jnp.where(pick, gate[e : e + 1, :], 0.0), axis=1, keepdims=True)
            )
        left = jnp.concatenate(picks, axis=0)
        scale = jnp.concatenate(scales, axis=0)
        left = jnp.concatenate([left, left], axis=1)
        sent = lax.dot_general(left, right, NT, preferred_element_type=F32) * scale
        sent = sent.astype(BF16)
        source = pl.multiple_of(lax.bitwise_xor(me, k) * cap, cap)
        for e in range(exp_local):
            a_ref[e, pl.ds(source, cap), :] = sent[e * cap : (e + 1) * cap, :]
    wide = DOC_GRP * half
    lane = lax.broadcasted_iota(jnp.int32, (wide, 2 * rank), 1)
    for e in range(exp_local):
        feat = lax.dot_general(a_ref[e], low_ref[e], TN, preferred_element_type=F32)
        f_ref[pl.ds(e, wide, stride=exp_local), :] = jnp.where(
            lane < rank, feat[:wide], feat[wide:]
        )
    _, chunks, _, _ = outs[0].shape
    size = chunks * exp_local
    for k in range(parts):
        part = lax.bitwise_xor(mine_ref[0], k)
        for d in range(DOC_GRP):
            start = pl.multiple_of((d * half + part * chunks) * exp_local, size)
            outs[k][d] = (
                f_ref[pl.ds(start, size), :].astype(BF16).reshape(chunks, exp_local, 2 * rank)
            )


def score_kernel(parts, scale, mine_ref, *refs):
    feats, pieces, out_ref = refs[:parts], refs[parts:-1], refs[-1]
    docs, chunks, exp_local, lanes = feats[0].shape
    each = pieces[0].shape[0]
    vals = len(pieces) * each
    left_rows, right_rows = parts * docs * exp_local, vals * exp_local
    total = jnp.zeros((left_rows, right_rows), F32)
    for c in range(chunks):
        left = jnp.concatenate(
            [feat[:, c].reshape(docs * exp_local, lanes) for feat in feats], axis=0
        )
        right = jnp.concatenate(
            [
                val[:, :, c * lanes : (c + 1) * lanes].reshape(each * exp_local, lanes)
                for val in pieces
            ],
            axis=0,
        )
        total += lax.dot_general(left, right, NT, preferred_element_type=F32)
    row = lax.broadcasted_iota(jnp.int32, total.shape, 0) % exp_local
    col = lax.broadcasted_iota(jnp.int32, total.shape, 1) % exp_local
    total = jnp.where(row == col, total, 0.0)
    total = jnp.sum(total.reshape(parts * docs, exp_local, right_rows), axis=1)
    owner = lax.broadcasted_iota(jnp.int32, (right_rows, vals), 0) // exp_local
    owner = lax.bitwise_xor(owner, mine_ref[0] * each)
    pick = (owner == lax.broadcasted_iota(jnp.int32, (right_rows, vals), 1)).astype(F32)
    scores = jnp.dot(
        total, pick, preferred_element_type=F32, precision=lax.Precision.HIGHEST
    ) * scale
    for k in range(parts):
        group = lax.bitwise_xor(mine_ref[0] % parts, k)
        for i in range(out_ref.shape[0] // parts):
            out_ref[i * parts + group] = scores[k * docs : (k + 1) * docs, :]


def layer(tokens, gates, routes, doc_ids, hidden_grad, proj_in, proj_out, val_features):
    tok, width = tokens.shape
    top = routes.shape[1]
    rank = proj_in.shape[1]
    groups = lax.axis_size("expert")
    lo = lax.axis_size("lo")
    dp = lax.axis_size("hi") * lo
    exp_local, rows, hidden = hidden_grad.shape
    vals = val_features.shape[0]
    entries = rank * rank
    experts = exp_local * groups
    chunks = entries // LANES // lo

    vmem = pl.BlockSpec(memory_space=pltpu.VMEM)
    hbm = pl.BlockSpec(memory_space=pltpu.HBM)
    smem = pl.BlockSpec(memory_space=pltpu.SMEM)
    mine = lax.axis_index("lo").astype(jnp.int32).reshape(1)
    piece = entries // lo
    pieces = [
        lax.dynamic_slice_in_dim(val_features, lax.bitwise_xor(mine[0], k) * piece, piece, 2)
        for k in range(lo)
    ]
    val_all = [pieces[0]] * dp
    for k in start_order(dp, lo):
        val_all[k] = lax.ppermute(
            pieces[k % lo], ("hi", "lo"), [(a, a ^ k) for a in range(dp)]
        )

    pay_rows = rank + 2 * top + 8
    steps = 1
    pay = pl.pallas_call(
        act_kernel,
        out_shape=jax.ShapeDtypeStruct((pay_rows, tok), F32),
        in_specs=[hbm] * 5,
        out_specs=vmem,
        scratch_shapes=[
            pltpu.VMEM((tok, width), BF16),
            pltpu.VMEM((rank, width), BF16),
            pltpu.VMEM((top, tok), jnp.int32),
            pltpu.VMEM((top, tok), F32),
            pltpu.VMEM((1, tok), jnp.int32),
            pltpu.VMEM((rank, tok), F32),
            pltpu.SemaphoreType.DMA((steps, 2)),
            pltpu.SemaphoreType.DMA((3,)),
        ],
        compiler_params=pltpu.CompilerParams(vmem_limit_bytes=VL_A),
        cost_estimate=pl.CostEstimate(
            flops=2 * tok * width * rank,
            bytes_accessed=2 * width * (tok + rank),
            transcendentals=0,
        ),
    )(tokens, proj_in.T, routes.T, gates.T, doc_ids.reshape(1, tok))

    pays = [pay]
    for k in range(1, groups):
        pays.append(lax.ppermute(pay, "expert", [(a, a ^ k) for a in range(groups)]))

    low = pl.pallas_call(
        lowered_kernel,
        out_shape=jax.ShapeDtypeStruct((exp_local, rows, 2 * rank), BF16),
        in_specs=[hbm, hbm],
        out_specs=vmem,
        scratch_shapes=[
            pltpu.VMEM((exp_local, rows, hidden), BF16),
            pltpu.VMEM((exp_local, rank, hidden), BF16),
            pltpu.SemaphoreType.DMA((4, 2)),
        ],
        compiler_params=pltpu.CompilerParams(vmem_limit_bytes=VL_L),
        cost_estimate=pl.CostEstimate(
            flops=2 * exp_local * rows * hidden * rank,
            bytes_accessed=2 * exp_local * hidden * (rows + rank),
            transcendentals=0,
        ),
    )(hidden_grad, proj_out.transpose(0, 2, 1))

    me = lax.axis_index("expert").astype(jnp.int32).reshape(1)
    block = jax.ShapeDtypeStruct((DOC_GRP, chunks, exp_local, LANES), BF16)
    feats = pl.pallas_call(
        functools.partial(feature_kernel, groups, lo, rank, top),
        out_shape=(block,) * lo,
        in_specs=[smem, smem] + [vmem] * (groups + 1),
        out_specs=(vmem,) * lo,
        scratch_shapes=[
            pltpu.VMEM((exp_local, rows, 2 * rank), BF16),
            pltpu.VMEM((DOC_GRP * rank // 2 * exp_local, 2 * rank), F32),
        ],
        compiler_params=pltpu.CompilerParams(vmem_limit_bytes=VL_F),
        cost_estimate=pl.CostEstimate(
            flops=8 * exp_local * rows * rank * tok, bytes_accessed=1 << 20, transcendentals=0
        ),
    )(me, mine, *pays, low)
    arrived = [feats[0]] * lo
    for k in range(lo - 1, 0, -1):
        arrived[k] = lax.ppermute(feats[k], "lo", [(a, a ^ k) for a in range(lo)])

    scale = 1.0 / float(experts * entries) ** 0.5
    part = pl.pallas_call(
        functools.partial(score_kernel, lo, scale),
        out_shape=jax.ShapeDtypeStruct((groups * lo, DOC_GRP, dp * vals), F32),
        in_specs=[smem] + [vmem] * (lo + dp),
        out_specs=vmem,
        compiler_params=pltpu.CompilerParams(vmem_limit_bytes=40 << 20),
    )(lax.axis_index(("hi", "lo")).astype(jnp.int32).reshape(1), *arrived, *val_all)
    parts = lax.all_to_all(part, ("expert", "lo"), split_axis=0, concat_axis=0, tiled=True)
    return jnp.sum(parts, axis=0)


def solution(mesh):
    groups, dp = mesh.shape["expert"], mesh.shape["dp"]
    lo = min(SPLIT, dp)
    grid = Mesh(mesh.devices.reshape(groups, dp // lo, lo), ("expert", "hi", "lo"))
    everyone = ("expert", "hi", "lo")
    in_specs = (
        P(everyone, None),
        P(everyone, None),
        P(everyone, None),
        P(everyone),
        P("expert", ("hi", "lo"), None),
        P(),
        P("expert", None, None),
        P(("hi", "lo"), "expert", None),
    )
    out_specs = P(("hi", "lo"), None)
    return jax.shard_map(layer, mesh=grid, in_specs=in_specs, out_specs=out_specs, check_vma=False)
```

```python
import functools

import jax
import jax.numpy as jnp
from jax import lax
from jax.experimental import pallas as pl
from jax.experimental.pallas import tpu as pltpu
from jax.sharding import Mesh
from jax.sharding import PartitionSpec as P


DOC_GRP = 2
SPLIT = 4
LANES = 128
VL_A = 63 << 20
VL_L = 53 << 20
VL_F = 16 << 20
F32 = jnp.float32
BF16 = jnp.bfloat16
NT = (((1,), (1,)), ((), ()))
TN = (((0,), (0,)), ((), ()))


def start_order(dp, lo):
    return sorted(range(dp - 1, 0, -1), key=lambda k: (k < lo, k % 2 if k >= lo else 0))


def split_kernel(mine_ref, val_hbm, *refs):
    outs, (piece_ref, sems) = refs[:-2], refs[-2:]
    parts, _, _, piece = piece_ref.shape
    ins, puts = [], []
    for k in range(parts):
        part = lax.bitwise_xor(mine_ref[0], k)
        cols = pl.ds(pl.multiple_of(part * piece, piece), piece)
        ins.append(pltpu.make_async_copy(val_hbm.at[:, :, cols], piece_ref.at[k], sems.at[k, 0]))
        puts.append(pltpu.make_async_copy(piece_ref.at[k], outs[k], sems.at[k, 1]))
    for copy in ins:
        copy.start()
    for k in range(parts):
        ins[k].wait()
        puts[k].start()
    for copy in puts:
        copy.wait()


def act_kernel(tok_hbm, proj_hbm, routes_hbm, gates_hbm, docs_hbm, out_ref, *scratch):
    tok_ref, proj_ref, routes_ref, gates_ref, docs_ref, acc_ref, sems, small_sems = scratch
    rank = proj_ref.shape[0]
    top = routes_ref.shape[0]
    half = rank // 2
    steps = sems.shape[0]
    width = tok_ref.shape[1] // steps
    copies = []
    for s in range(steps):
        cols = pl.ds(s * width, width)
        copies.append(
            (
                pltpu.make_async_copy(proj_hbm.at[:, cols], proj_ref.at[:, cols], sems.at[s, 0]),
                pltpu.make_async_copy(tok_hbm.at[:, cols], tok_ref.at[:, cols], sems.at[s, 1]),
            )
        )
    smalls = [
        pltpu.make_async_copy(routes_hbm, routes_ref, small_sems.at[0]),
        pltpu.make_async_copy(gates_hbm, gates_ref, small_sems.at[1]),
        pltpu.make_async_copy(docs_hbm, docs_ref, small_sems.at[2]),
    ]
    for copy in copies[0]:
        copy.start()
    for copy in smalls:
        copy.start()
    for pair in copies[1:]:
        for copy in pair:
            copy.start()
    for copy in smalls:
        copy.wait()
    out_ref[rank : rank + top, :] = routes_ref[...].astype(F32)
    out_ref[rank + top : rank + 2 * top, :] = gates_ref[...]
    out_ref[rank + 2 * top :, :] = jnp.broadcast_to(
        docs_ref[...].astype(F32), (out_ref.shape[0] - rank - 2 * top, out_ref.shape[1])
    )
    total = jnp.zeros(acc_ref.shape, F32)
    for s in range(steps):
        for copy in copies[s]:
            copy.wait()
        cols = slice(s * width, (s + 1) * width)
        total += lax.dot_general(
            proj_ref[:, cols], tok_ref[:, cols], NT, preferred_element_type=F32
        )
    acc_ref[...] = total
    out_ref[0:half, :] = acc_ref[pl.ds(0, half, stride=2), :]
    out_ref[half:rank, :] = acc_ref[pl.ds(1, half, stride=2), :]


def lowered_kernel(grad_hbm, proj_hbm, out_ref, grad_ref, proj_ref, sems):
    count = sems.shape[0]
    batch = grad_ref.shape[0] // count
    copies = []
    for n in range(count):
        part = pl.ds(n * batch, batch)
        copies.append(
            (
                pltpu.make_async_copy(proj_hbm.at[part], proj_ref.at[part], sems.at[n, 0]),
                pltpu.make_async_copy(grad_hbm.at[part], grad_ref.at[part], sems.at[n, 1]),
            )
        )
    for pair in copies:
        for copy in pair:
            copy.start()
    for n in range(count):
        for copy in copies[n]:
            copy.wait()
        for e in range(n * batch, (n + 1) * batch):
            low = lax.dot_general(grad_ref[e], proj_ref[e], NT, preferred_element_type=F32)
            out_ref[e] = jnp.concatenate([low, low], axis=1).astype(BF16)


def feature_kernel(groups, parts, rank, top, me_ref, mine_ref, *refs):
    pays = refs[:groups]
    low_ref = refs[groups]
    outs = refs[groups + 1 : groups + 1 + parts]
    a_ref, f_ref = refs[groups + 1 + parts :]
    exp_local, rows, _ = low_ref.shape
    cap = rows // groups
    tok = pays[0].shape[1]
    half = rank // 2
    me = me_ref[0]
    base = (me * exp_local).astype(F32)
    experts = lax.broadcasted_iota(jnp.int32, (exp_local, tok), 0).astype(F32) + base
    before = (
        lax.broadcasted_iota(jnp.int32, (tok, tok), 0)
        < lax.broadcasted_iota(jnp.int32, (tok, tok), 1)
    ).astype(BF16)
    slots = lax.broadcasted_iota(jnp.int32, (cap, tok), 0).astype(F32)
    for k in range(groups):
        pay = pays[k]
        hit = jnp.zeros((exp_local, tok), F32)
        gate = jnp.zeros((exp_local, tok), F32)
        for t in range(top):
            same = pay[rank + t : rank + t + 1, :] == experts
            hit = jnp.where(same, 1.0, hit)
            gate = jnp.where(same, pay[rank + top + t : rank + top + t + 1, :], gate)
        slot = jnp.dot(hit.astype(BF16), before, preferred_element_type=F32)
        slot = jnp.where(hit > 0.0, slot, -1.0)
        doc = pay[rank + 2 * top : rank + 2 * top + 1, :]
        masked = []
        for par in range(2):
            act = pay[par * half : (par + 1) * half, :]
            for d in range(DOC_GRP):
                masked.append(jnp.where(doc == float(d), act, 0.0))
        act = jnp.concatenate(masked, axis=0)
        high = act.astype(BF16)
        low = (act - high.astype(F32)).astype(BF16)
        right = jnp.concatenate([high, low], axis=1)
        picks, scales = [], []
        for e in range(exp_local):
            pick = slot[e : e + 1, :] == slots
            picks.append(jnp.where(pick, 1.0, 0.0).astype(BF16))
            scales.append(
                jnp.sum(jnp.where(pick, gate[e : e + 1, :], 0.0), axis=1, keepdims=True)
            )
        left = jnp.concatenate(picks, axis=0)
        scale = jnp.concatenate(scales, axis=0)
        left = jnp.concatenate([left, left], axis=1)
        sent = lax.dot_general(left, right, NT, preferred_element_type=F32) * scale
        sent = sent.astype(BF16)
        source = pl.multiple_of(lax.bitwise_xor(me, k) * cap, cap)
        for e in range(exp_local):
            a_ref[e, pl.ds(source, cap), :] = sent[e * cap : (e + 1) * cap, :]
    wide = DOC_GRP * half
    lane = lax.broadcasted_iota(jnp.int32, (wide, 2 * rank), 1)
    for e in range(exp_local):
        feat = lax.dot_general(a_ref[e], low_ref[e], TN, preferred_element_type=F32)
        f_ref[pl.ds(e, wide, stride=exp_local), :] = jnp.where(
            lane < rank, feat[:wide], feat[wide:]
        )
    _, chunks, _, _ = outs[0].shape
    size = chunks * exp_local
    for k in range(parts):
        part = lax.bitwise_xor(mine_ref[0], k)
        for d in range(DOC_GRP):
            start = pl.multiple_of((d * half + part * chunks) * exp_local, size)
            outs[k][d] = (
                f_ref[pl.ds(start, size), :].astype(BF16).reshape(chunks, exp_local, 2 * rank)
            )


def score_kernel(parts, scale, mine_ref, *refs):
    feats, pieces, out_ref = refs[:parts], refs[parts:-1], refs[-1]
    docs, chunks, exp_local, lanes = feats[0].shape
    each = pieces[0].shape[0]
    vals = len(pieces) * each
    left_rows, right_rows = parts * docs * exp_local, vals * exp_local
    total = jnp.zeros((left_rows, right_rows), F32)
    for c in range(chunks):
        left = jnp.concatenate(
            [feat[:, c].reshape(docs * exp_local, lanes) for feat in feats], axis=0
        )
        right = jnp.concatenate(
            [
                val[:, :, c * lanes : (c + 1) * lanes].reshape(each * exp_local, lanes)
                for val in pieces
            ],
            axis=0,
        )
        total += lax.dot_general(left, right, NT, preferred_element_type=F32)
    row = lax.broadcasted_iota(jnp.int32, total.shape, 0) % exp_local
    col = lax.broadcasted_iota(jnp.int32, total.shape, 1) % exp_local
    total = jnp.where(row == col, total, 0.0)
    total = jnp.sum(total.reshape(parts * docs, exp_local, right_rows), axis=1)
    owner = lax.broadcasted_iota(jnp.int32, (right_rows, vals), 0) // exp_local
    owner = lax.bitwise_xor(owner, mine_ref[0] * each)
    pick = (owner == lax.broadcasted_iota(jnp.int32, (right_rows, vals), 1)).astype(F32)
    scores = jnp.dot(
        total, pick, preferred_element_type=F32, precision=lax.Precision.HIGHEST
    ) * scale
    for k in range(parts):
        group = lax.bitwise_xor(mine_ref[0] % parts, k)
        for i in range(out_ref.shape[0] // parts):
            out_ref[i * parts + group] = scores[k * docs : (k + 1) * docs, :]


def layer(tokens, gates, routes, doc_ids, hidden_grad, proj_in, proj_out, val_features):
    tok, width = tokens.shape
    top = routes.shape[1]
    rank = proj_in.shape[1]
    groups = lax.axis_size("expert")
    lo = lax.axis_size("lo")
    dp = lax.axis_size("hi") * lo
    exp_local, rows, hidden = hidden_grad.shape
    vals = val_features.shape[0]
    entries = rank * rank
    experts = exp_local * groups
    chunks = entries // LANES // lo

    vmem = pl.BlockSpec(memory_space=pltpu.VMEM)
    hbm = pl.BlockSpec(memory_space=pltpu.HBM)
    smem = pl.BlockSpec(memory_space=pltpu.SMEM)
    mine = lax.axis_index("lo").astype(jnp.int32).reshape(1)
    pieces = pl.pallas_call(
        split_kernel,
        out_shape=(jax.ShapeDtypeStruct((vals, exp_local, entries // lo), BF16),) * lo,
        in_specs=[smem, hbm],
        out_specs=(hbm,) * lo,
        scratch_shapes=[
            pltpu.VMEM((lo, vals, exp_local, entries // lo), BF16),
            pltpu.SemaphoreType.DMA((lo, 2)),
        ],
        compiler_params=pltpu.CompilerParams(vmem_limit_bytes=VL_A),
    )(mine, val_features)
    val_all = [pieces[0]] * dp
    for k in start_order(dp, lo):
        val_all[k] = lax.ppermute(
            pieces[k % lo], ("hi", "lo"), [(a, a ^ k) for a in range(dp)]
        )

    pay_rows = rank + 2 * top + 8
    steps = 2
    pay = pl.pallas_call(
        act_kernel,
        out_shape=jax.ShapeDtypeStruct((pay_rows, tok), F32),
        in_specs=[hbm] * 5,
        out_specs=vmem,
        scratch_shapes=[
            pltpu.VMEM((tok, width), BF16),
            pltpu.VMEM((rank, width), BF16),
            pltpu.VMEM((top, tok), jnp.int32),
            pltpu.VMEM((top, tok), F32),
            pltpu.VMEM((1, tok), jnp.int32),
            pltpu.VMEM((rank, tok), F32),
            pltpu.SemaphoreType.DMA((steps, 2)),
            pltpu.SemaphoreType.DMA((3,)),
        ],
        compiler_params=pltpu.CompilerParams(vmem_limit_bytes=VL_A),
        cost_estimate=pl.CostEstimate(
            flops=2 * tok * width * rank,
            bytes_accessed=2 * width * (tok + rank),
            transcendentals=0,
        ),
    )(tokens, proj_in.T, routes.T, gates.T, doc_ids.reshape(1, tok))

    pays = [pay]
    for k in range(1, groups):
        pays.append(lax.ppermute(pay, "expert", [(a, a ^ k) for a in range(groups)]))

    low = pl.pallas_call(
        lowered_kernel,
        out_shape=jax.ShapeDtypeStruct((exp_local, rows, 2 * rank), BF16),
        in_specs=[hbm, hbm],
        out_specs=vmem,
        scratch_shapes=[
            pltpu.VMEM((exp_local, rows, hidden), BF16),
            pltpu.VMEM((exp_local, rank, hidden), BF16),
            pltpu.SemaphoreType.DMA((2, 2)),
        ],
        compiler_params=pltpu.CompilerParams(vmem_limit_bytes=VL_L),
        cost_estimate=pl.CostEstimate(
            flops=2 * exp_local * rows * hidden * rank,
            bytes_accessed=2 * exp_local * hidden * (rows + rank),
            transcendentals=0,
        ),
    )(hidden_grad, proj_out.transpose(0, 2, 1))

    me = lax.axis_index("expert").astype(jnp.int32).reshape(1)
    block = jax.ShapeDtypeStruct((DOC_GRP, chunks, exp_local, LANES), BF16)
    feats = pl.pallas_call(
        functools.partial(feature_kernel, groups, lo, rank, top),
        out_shape=(block,) * lo,
        in_specs=[smem, smem] + [vmem] * (groups + 1),
        out_specs=(vmem,) * lo,
        scratch_shapes=[
            pltpu.VMEM((exp_local, rows, 2 * rank), BF16),
            pltpu.VMEM((DOC_GRP * rank // 2 * exp_local, 2 * rank), F32),
        ],
        compiler_params=pltpu.CompilerParams(vmem_limit_bytes=VL_F),
        cost_estimate=pl.CostEstimate(
            flops=8 * exp_local * rows * rank * tok, bytes_accessed=1 << 20, transcendentals=0
        ),
    )(me, mine, *pays, low)
    arrived = [feats[0]] * lo
    for k in range(lo - 1, 0, -1):
        arrived[k] = lax.ppermute(feats[k], "lo", [(a, a ^ k) for a in range(lo)])

    scale = 1.0 / float(experts * entries) ** 0.5
    part = pl.pallas_call(
        functools.partial(score_kernel, lo, scale),
        out_shape=jax.ShapeDtypeStruct((groups * lo, DOC_GRP, dp * vals), F32),
        in_specs=[smem] + [vmem] * (lo + dp),
        out_specs=vmem,
        compiler_params=pltpu.CompilerParams(vmem_limit_bytes=40 << 20),
    )(lax.axis_index(("hi", "lo")).astype(jnp.int32).reshape(1), *arrived, *val_all)
    parts = lax.all_to_all(part, ("expert", "lo"), split_axis=0, concat_axis=0, tiled=True)
    return jnp.sum(parts, axis=0)


def solution(mesh):
    groups, dp = mesh.shape["expert"], mesh.shape["dp"]
    lo = min(SPLIT, dp)
    grid = Mesh(mesh.devices.reshape(groups, dp // lo, lo), ("expert", "hi", "lo"))
    everyone = ("expert", "hi", "lo")
    in_specs = (
        P(everyone, None),
        P(everyone, None),
        P(everyone, None),
        P(everyone),
        P("expert", ("hi", "lo"), None),
        P(),
        P("expert", None, None),
        P(("hi", "lo"), "expert", None),
    )
    out_specs = P(("hi", "lo"), None)
    return jax.shard_map(layer, mesh=grid, in_specs=in_specs, out_specs=out_specs, check_vma=False)
```
